128 devices in a mesh: gx: 16 (over z, x_hi, core), gy: 8 (over x_lo, y).
Axes of the slice: x: 4 (x_hi: 2, x_lo: 2; x = x_hi * 2 + x_lo), y: 4, z: 4, core: 2. Of those that a mesh axis runs over, the one named last changes fastest.
Arguments:
- grid_field: bfloat16 [1, 20, 2048, 2048], P(None, None, 'gx', 'gy'), may hold values from -8 to 8
- spectral_weight: float32 [2, 2, 20, 20, 2048], P(None, None, None, None, ('gx', 'gy')), may hold values from -1 to 1
- conv_near: bfloat16 [2, 20, 180], replicated, may hold values from -0.4375 to 0.4375
- conv_far: bfloat16 [2, 20, 500], replicated, may hold values from -0.25 to 0.25
- mix_logits: float32 [2, 3], replicated, may hold values from -1 to 1
- channel_bias: float32 [2, 20], replicated, may hold values from -3 to 3
Outputs:
- result_field: bfloat16 [1, 20, 2048, 2048], P(None, None, 'gx', 'gy')
The draws below stay inside these ranges and needn't reach their ends.
All inputs are finite; a program needn't handle non-finite values.
Results may differ from the reference program's by a relative error of at most 0.004.
Values may be sent and summed in bfloat16 or wider, within the bound.
No kernel may reach another device: no remote copies, remote signals or barrier semaphores. Data moves between devices by JAX's collectives and lax.ppermute only.
A program may use at most 192 MiB of HBM per device.

```python
import math
import jax
import jax.numpy as jnp
from jax import lax

NX = 2048
NY = 2048
C = 20
MX = 32
MY = 32
LAYERS = 2
PLANES = 1
KX = 64
MODES = 2048


def wave_profile(sub_key, length, highest_mode):
    sub_keys = jax.random.split(sub_key, 2)
    frequency = jnp.arange(highest_mode, dtype=jnp.int32)
    amplitude = jax.random.normal(sub_keys[0], (PLANES, C, highest_mode, 1), jnp.float32) * math.sqrt(2.0 / highest_mode)
    phases = jax.random.uniform(sub_keys[1], (PLANES, C, highest_mode, 1), jnp.float32, 0.0, 2.0 * math.pi)
    positions = jnp.arange(length, dtype=jnp.int32)
    angle_grid = (frequency[:, None] * positions[None, :] % length).astype(jnp.float32) * (2.0 * math.pi / length)
    return jnp.sum(amplitude * jnp.cos(angle_grid[None, None, :, :] + phases), axis=2)


def draw_grid_field(key, part):
    noise_key, first_key, second_key = jax.random.split(jax.random.fold_in(key, 17), 3)
    roughness = jax.random.normal(noise_key, (PLANES, C, NX, NY), jnp.float32)
    profile_rows = wave_profile(first_key, NX, MX)
    profile_cols = wave_profile(second_key, NY, MY)
    smooth = profile_rows[:, :, :, None] * profile_cols[:, :, None, :]
    return jnp.clip(roughness + smooth, -8.0, 8.0).astype(jnp.bfloat16)


def level_of(stream_key, shape, cuts, low, largest):
    factor_of = 1.0
    for dim, shards_of in cuts:
        steps = jax.random.uniform(jax.random.fold_in(jax.random.fold_in(stream_key, 6), dim), (shards_of,), jnp.float32, low / len(cuts), largest / len(cuts))
        factor_of = factor_of * jnp.repeat(jnp.exp(steps), shape[dim] // shards_of).reshape((-1,) + (1,) * (len(shape) - 1 - dim))
    return factor_of


def scatter_about(rng, extent, deviation, reach, pieces=(), kind=jnp.bfloat16):
    values = jax.random.normal(rng, extent, jnp.float32) * deviation
    if len(pieces) > 0:
        values = level_of(rng, extent, pieces, -0.22, 0.18) * values
    return jnp.clip(values, min=-reach, max=reach).astype(kind)


def setup_inputs(seed: int = 0) -> dict:
    streams_of = jax.random.split(jax.random.key(seed), 7)
    grid_field = draw_grid_field(jax.random.fold_in(streams_of[6], 71), 0)
    spectral_weight = scatter_about(streams_of[1], (LAYERS, 2, C, C, MODES), (2 * C) ** -0.5, 1.0, ((4, 128),), jnp.float32)
    conv_near = scatter_about(streams_of[2], (LAYERS, C, 9 * C), (9 * C) ** -0.5, 0.4375)
    conv_far = scatter_about(streams_of[3], (LAYERS, C, 25 * C), (25 * C) ** -0.5, 0.25)
    mix_logits = jnp.clip(jax.random.uniform(streams_of[4], (LAYERS, 3), jnp.float32, -1.0, 1.0), -1.0, 1.0)
    channel_bias = scatter_about(streams_of[5], (LAYERS, C), 0.5, 3.0, (), jnp.float32)
    return {"grid_field": grid_field, "spectral_weight": spectral_weight, "conv_near": conv_near, "conv_far": conv_far, "mix_logits": mix_logits, "channel_bias": channel_bias}


full_turn = 2.0 * math.pi
highest = lax.Precision.HIGHEST


def forward_table(positions):
    col_modes = jnp.arange(MY, dtype=jnp.int32)
    phases = ((positions[:, None] * col_modes[None, :]) % NY).astype(jnp.float32) * (full_turn / NY)
    return jnp.concatenate([jnp.cos(phases), -jnp.sin(phases)], axis=1).astype(jnp.bfloat16)


def row_tables(positions):
    lower = jnp.arange(MX, dtype=jnp.int32)
    row_modes = jnp.concatenate([lower, lower + (NX - MX)])
    phases = ((positions[:, None] * row_modes[None, :]) % NX).astype(jnp.float32) * (full_turn / NX)
    return jnp.cos(phases), jnp.sin(phases)


def inverse_table(positions):
    col_modes = jnp.arange(MY, dtype=jnp.int32)
    col_weight = jnp.where(col_modes == 0, 1.0, 2.0).astype(jnp.float32) / (NX * NY)
    phases = ((col_modes[:, None] * positions[None, :]) % NY).astype(jnp.float32) * (full_turn / NY)
    return jnp.concatenate([jnp.cos(phases) * col_weight[:, None], -jnp.sin(phases) * col_weight[:, None]], axis=0)


def block_height():
    height = min(NX, 128)
    while NX % height != 0:
        height = height - 1
    return height


def mixed_spectrum(plane_field, weight_pair, forward_cols, cosine_rows, sine_rows):
    channels = plane_field.shape[0]
    line_sums = jnp.dot(plane_field.reshape(channels * NX, NY), forward_cols, preferred_element_type=jnp.float32)
    line_sums = line_sums.reshape(channels, NX, 2 * MY)
    real_lines = line_sums[..., :MY]
    imaginary_lines = line_sums[..., MY:]

    def contract_rows(operand, lookup):
        return jnp.einsum("cxk,xj->cjk", operand, lookup, precision=highest)

    real_spec = (contract_rows(real_lines, cosine_rows) + contract_rows(imaginary_lines, sine_rows)).reshape(channels, MODES)
    imaginary_spec = (contract_rows(imaginary_lines, cosine_rows) - contract_rows(real_lines, sine_rows)).reshape(channels, MODES)

    def mix_modes(spectrum, weights):
        return jnp.einsum("cm,com->om", spectrum, weights, precision=highest)

    real_mixed = mix_modes(real_spec, weight_pair[0]) - mix_modes(imaginary_spec, weight_pair[1])
    imaginary_mixed = mix_modes(imaginary_spec, weight_pair[0]) + mix_modes(real_spec, weight_pair[1])
    return real_mixed.reshape(channels, KX, MY), imaginary_mixed.reshape(channels, KX, MY)


def conv_block(padded_rows, tap_weights, dilation, side_taps, height):
    channels = padded_rows.shape[0]
    accumulated = jnp.zeros((channels, height * NY), jnp.float32)
    for tap_index in range(side_taps * side_taps):
        shift_row = (tap_index // side_taps - side_taps // 2) * dilation
        shift_col = (tap_index % side_taps - side_taps // 2) * dilation
        piece = padded_rows[:, 4 + shift_row:4 + shift_row + height, 4 + shift_col:4 + shift_col + NY]
        piece = piece.astype(jnp.float32).reshape(channels, height * NY)
        weights_tap = tap_weights[:, tap_index * channels:(tap_index + 1) * channels].astype(jnp.float32)
        accumulated = accumulated + jnp.dot(weights_tap, piece, precision=highest)
    return accumulated.reshape(channels, height, NY)


def reference(grid_field, spectral_weight, conv_near, conv_far, mix_logits, channel_bias):
    row_positions = jnp.arange(NX, dtype=jnp.int32)
    col_positions = jnp.arange(NY, dtype=jnp.int32)
    cosine_rows, sine_rows = row_tables(row_positions)
    forward_cols = forward_table(col_positions)
    inverse_cols = inverse_table(col_positions)
    height = block_height()
    block_starts = jnp.arange(NX // height, dtype=jnp.int32) * height

    def per_plane(plane_field):
        channels = plane_field.shape[0]
        for layer_index in range(LAYERS):
            real_mixed, imaginary_mixed = mixed_spectrum(plane_field, spectral_weight[layer_index], forward_cols, cosine_rows, sine_rows)
            padded = jnp.pad(plane_field, ((0, 0), (4, 4), (4, 4)), mode="wrap")
            exponents = jnp.exp(mix_logits[layer_index])
            mixture = exponents / jnp.sum(exponents)
            bias_column = channel_bias[layer_index][:, None, None]
            near_weights = conv_near[layer_index]
            far_weights = conv_far[layer_index]

            def per_block(start):
                cos_block = lax.dynamic_slice_in_dim(cosine_rows, start, height, 0)
                sin_block = lax.dynamic_slice_in_dim(sine_rows, start, height, 0)

                def expand_rows(spectrum, lookup):
                    return jnp.einsum("cjk,xj->cxk", spectrum, lookup, precision=highest)

                real_rows = expand_rows(real_mixed, cos_block) - expand_rows(imaginary_mixed, sin_block)
                imaginary_rows = expand_rows(real_mixed, sin_block) + expand_rows(imaginary_mixed, cos_block)
                stacked = jnp.concatenate([real_rows, imaginary_rows], axis=-1).reshape(channels * height, 2 * MY)
                spectral = jnp.dot(stacked, inverse_cols, precision=highest).reshape(channels, height, NY)
                padded_rows = lax.dynamic_slice_in_dim(padded, start, height + 8, 1)
                near_term = conv_block(padded_rows, near_weights, 1, 3, height)
                far_term = conv_block(padded_rows, far_weights, 2, 5, height)
                summed = mixture[0] * spectral + mixture[1] * near_term + mixture[2] * far_term + bias_column
                return jax.nn.gelu(summed, approximate=False).astype(jnp.bfloat16)

            blocks = lax.map(per_block, block_starts)
            plane_field = jnp.transpose(blocks, (1, 0, 2, 3)).reshape(channels, NX, NY)
        return plane_field

    return lax.map(per_plane, grid_field)
```

```python
import math

import jax
import jax.numpy as jnp
from jax import lax
from jax.sharding import PartitionSpec as P

NX = 2048
NY = 2048
MX = 32
MY = 32
LAYERS = 2
KX = 64
MODES = 2048


full_turn = 2.0 * math.pi
highest = lax.Precision.HIGHEST


def padded_2(value, sides, width):
    for axis, dim in sides:
        size, length = (lax.axis_size(axis), value.shape[dim])
        up = [(i, (i + 1) % size) for i in range(size)]
        down = [(j, i) for i, j in up]
        last = lax.slice_in_dim(value, length - width, length, axis=dim)
        first = lax.slice_in_dim(value, 0, width, axis=dim)
        before = lax.ppermute(last, axis, up)
        after = lax.ppermute(first, axis, down)
        value = jnp.concatenate([before, value, after], axis=dim)
    return value


def forward_table(positions):
    col_modes = jnp.arange(MY, dtype=jnp.int32)
    phases = (positions[:, None] * col_modes[None, :] % NY).astype(jnp.float32) * (full_turn / NY)
    return jnp.concatenate([jnp.cos(phases), -jnp.sin(phases)], axis=1).astype(jnp.bfloat16)


def row_tables(positions):
    lower = jnp.arange(MX, dtype=jnp.int32)
    row_modes = jnp.concatenate([lower, lower + (NX - MX)])
    phases = (positions[:, None] * row_modes[None, :] % NX).astype(jnp.float32) * (full_turn / NX)
    return (jnp.cos(phases), jnp.sin(phases))


def inverse_table(positions):
    col_modes = jnp.arange(MY, dtype=jnp.int32)
    col_weight = jnp.where(col_modes == 0, 1.0, 2.0).astype(jnp.float32) / (NX * NY)
    phases = (col_modes[:, None] * positions[None, :] % NY).astype(jnp.float32) * (full_turn / NY)
    return jnp.concatenate(
        [jnp.cos(phases) * col_weight[:, None], -jnp.sin(phases) * col_weight[:, None]], axis=0
    )


def conv_rows(padded_plane, tap_weights, dilation, side_taps, first_row, count_rows, local_cols):
    channels = padded_plane.shape[0]
    pieces = []
    for row_tap in range(side_taps):
        for col_tap in range(side_taps):
            row_offset = 4 + (row_tap - side_taps // 2) * dilation + first_row
            col_offset = 4 + (col_tap - side_taps // 2) * dilation
            pieces.append(
                padded_plane[
                    :, row_offset : row_offset + count_rows, col_offset : col_offset + local_cols
                ]
            )
    stacked = jnp.stack(pieces, 0)
    shaped_weights = tap_weights.reshape(channels, side_taps * side_taps, channels)
    return jnp.einsum("otc,tcxy->oxy", shaped_weights, stacked, preferred_element_type=jnp.float32)


def on_device(grid_field, spectral_weight, conv_near, conv_far, mix_logits, channel_bias):
    channels = grid_field.shape[1]
    local_rows = grid_field.shape[2]
    local_cols = grid_field.shape[3]
    row_positions = lax.axis_index("gx") * local_rows + jnp.arange(local_rows, dtype=jnp.int32)
    col_positions = lax.axis_index("gy") * local_cols + jnp.arange(local_cols, dtype=jnp.int32)
    forward_cols = forward_table(col_positions)
    cosine_rows, sine_rows = row_tables(row_positions)
    inverse_cols = inverse_table(col_positions)
    share_modes = spectral_weight.shape[-1]
    row_blocks = max(1, local_rows // 32)
    while local_rows % row_blocks != 0:
        row_blocks = row_blocks - 1
    block_rows = local_rows // row_blocks
    planes_block = grid_field
    for layer_index in range(LAYERS):
        planes_here = planes_block.shape[0]
        line_sums = jnp.dot(
            planes_block.reshape(planes_here * channels * local_rows, local_cols),
            forward_cols,
            preferred_element_type=jnp.float32,
        )
        line_sums = line_sums.reshape(planes_here, channels, local_rows, 2 * MY)
        real_lines = line_sums[..., :MY]
        imaginary_lines = line_sums[..., MY:]

        def contract_rows(operand, lookup):
            return jnp.einsum("pcxk,xj->pcjk", operand, lookup, precision=highest)

        real_spec = contract_rows(real_lines, cosine_rows) + contract_rows(
            imaginary_lines, sine_rows
        )
        imaginary_spec = contract_rows(imaginary_lines, cosine_rows) - contract_rows(
            real_lines, sine_rows
        )
        partial_value = jnp.stack(
            [
                real_spec.reshape(planes_here, channels, MODES),
                imaginary_spec.reshape(planes_here, channels, MODES),
            ]
        )
        devices = lax.axis_size("gx") * lax.axis_size("gy")
        blocks = partial_value.reshape(2 * channels, devices, share_modes)
        blocks = jnp.transpose(blocks, (1, 0, 2)).reshape(devices, 2 * channels * share_modes)
        received = lax.all_to_all(
            blocks.astype(jnp.bfloat16), ("gx", "gy"), split_axis=0, concat_axis=0, tiled=True
        )
        own_modes = jnp.sum(received.astype(jnp.float32), axis=0)
        own_modes = own_modes.reshape(2, planes_here, channels, share_modes)

        def mix_modes(spectrum, weights):
            return jnp.einsum("pcm,com->pom", spectrum, weights, precision=highest)

        weight_real = spectral_weight[layer_index, 0]
        weight_imaginary = spectral_weight[layer_index, 1]
        real_mixed = mix_modes(own_modes[0], weight_real) - mix_modes(
            own_modes[1], weight_imaginary
        )
        imaginary_mixed = mix_modes(own_modes[1], weight_real) + mix_modes(
            own_modes[0], weight_imaginary
        )
        own_block = jnp.stack([real_mixed, imaginary_mixed]).astype(jnp.bfloat16)
        copies = jnp.broadcast_to(
            own_block.reshape(1, 2 * channels * share_modes),
            (devices, 2 * channels * share_modes),
        )
        gathered = lax.all_to_all(copies, ("gx", "gy"), split_axis=0, concat_axis=0, tiled=True)
        gathered = gathered.astype(jnp.float32).reshape(devices, 2 * channels, share_modes)
        gathered = jnp.transpose(gathered, (1, 0, 2)).reshape(2, planes_here, channels, MODES)
        real_full = gathered[0].reshape(planes_here, channels, KX, MY)
        imaginary_full = gathered[1].reshape(planes_here, channels, KX, MY)

        def expand_rows(spectrum, lookup):
            return jnp.einsum("pcjk,xj->pcxk", spectrum, lookup, precision=highest)

        real_rows = expand_rows(real_full, cosine_rows) - expand_rows(imaginary_full, sine_rows)
        imaginary_rows = expand_rows(real_full, sine_rows) + expand_rows(
            imaginary_full, cosine_rows
        )
        stacked = jnp.concatenate([real_rows, imaginary_rows], axis=-1).reshape(
            planes_here * channels * local_rows, 2 * MY
        )
        spectral = jnp.dot(stacked, inverse_cols, precision=highest)
        layer_spectral = spectral.reshape(planes_here, channels, local_rows, local_cols)
        padded = padded_2(planes_block, (("gx", 2), ("gy", 3)), 4)
        exponents = jnp.exp(mix_logits[layer_index])
        mixture = exponents / jnp.sum(exponents)
        bias_column = channel_bias[layer_index][:, None, None]
        row_pieces = []
        for block_index in range(row_blocks):
            first_row = block_index * block_rows
            near_term = conv_rows(
                padded[0], conv_near[layer_index], 1, 3, first_row, block_rows, local_cols
            )
            far_term = conv_rows(
                padded[0], conv_far[layer_index], 2, 5, first_row, block_rows, local_cols
            )
            spectral_rows = layer_spectral[0, :, first_row : first_row + block_rows, :]
            summed = (
                mixture[0] * spectral_rows
                + mixture[1] * near_term
                + mixture[2] * far_term
                + bias_column
            )
            row_pieces.append(jax.nn.gelu(summed, approximate=False).astype(jnp.bfloat16))
        outputs = [jnp.concatenate(row_pieces, axis=1)]
        planes_block = jnp.stack(outputs)
    return planes_block


def solution(mesh):
    in_specs = (
        P(None, None, "gx", "gy"),
        P(None, None, None, None, ("gx", "gy")),
        P(),
        P(),
        P(),
        P(),
    )
    out_specs = P(None, None, "gx", "gy")
    return jax.shard_map(
        on_device, mesh=mesh, in_specs=in_specs, out_specs=out_specs, check_vma=False
    )
```

```python
import functools
import math

import jax
import jax.numpy as jnp
import ml_dtypes
import numpy as np
from jax import lax
from jax.experimental import pallas as pl
from jax.experimental.pallas import tpu as pltpu
from jax.sharding import PartitionSpec as P

NX = 2048
NY = 2048
C = 20
LAYERS = 2
ROWS = 128
COLS = 256
GROUPS = 5
WIDE = 384
BLOCK = 8 * C

f32 = jnp.float32
bf16 = jnp.bfloat16
both = ("gx", "gy")


def wave(numbers, positions, length):
    product = numbers.astype(np.int64)[:, None] * positions.astype(np.int64)[None, :]
    scale = np.float32(2.0 * math.pi / length)
    angle = (product % length).astype(np.float32) * scale
    angle = angle.astype(np.float64)
    return np.cos(angle).astype(np.float32), np.sin(angle).astype(np.float32)


def halves(value):
    high = value.astype(ml_dtypes.bfloat16)
    low = (value - high.astype(np.float32)).astype(ml_dtypes.bfloat16)
    return high, low


ky_all = np.arange(32)
kx_all = np.concatenate([np.arange(32), np.arange(32) + NX - 32])


def forward_cols():
    cosine, sine = wave(ky_all, np.arange(NY), NY)
    cosine, sine = cosine.T.reshape(NY, 2, 1, 16), sine.T.reshape(NY, 2, 1, 16)
    first = np.stack([cosine, -sine], axis=3)
    second = np.stack([-sine, -cosine], axis=3)
    tables = [np.broadcast_to(t, (NY, 2, 4, 2, 16)).reshape(NY, 256) for t in (first, second)]
    return np.stack(tables).astype(ml_dtypes.bfloat16)


def forward_rows(before, count):
    out = np.zeros((16, 2, 64, 2 * count), ml_dtypes.bfloat16)
    for device in range(16):
        cosine, sine = wave(kx_all, np.arange(ROWS) + device * ROWS, NX)
        table = np.zeros((2, 64, count), np.float32)
        table[0, :, before : before + ROWS] = cosine
        table[1, :, before : before + ROWS] = sine
        high, low = halves(np.transpose(table, (1, 0, 2)).reshape(64, 2 * count))
        out[device, 0], out[device, 1] = high, low
    return out


def inverse_rows(before, count):
    out = np.zeros((16, 2, count, 128), ml_dtypes.bfloat16)
    for device in range(16):
        positions = (np.arange(count) - before + device * ROWS) % NX
        cosine, sine = wave(kx_all, positions, NX)
        high, low = halves(np.concatenate([cosine.T, -sine.T], axis=1))
        out[device, 0], out[device, 1] = high, low
    return out


def inverse_cols(width):
    out = np.zeros((8, 2, 64, 2 * width), ml_dtypes.bfloat16)
    weight = (np.where(ky_all == 0, 1.0, 2.0) / (NX * NY)).astype(np.float32)[:, None]
    for device in range(8):
        lanes = np.arange(width)
        lanes = np.where(lanes >= 320, lanes - WIDE, lanes)
        cosine, sine = wave(ky_all, (lanes + device * COLS) % NY, NY)
        cosine, sine = cosine * weight, sine * weight
        real = np.concatenate([cosine, sine], axis=1)
        imaginary = np.concatenate([-sine, cosine], axis=1)
        table = np.stack([real.reshape(2, 16, 2 * width), imaginary.reshape(2, 16, 2 * width)], 1)
        high, low = halves(table.reshape(64, 2 * width))
        out[device, 0], out[device, 1] = high, low
    return out


def spread(taps):
    width = 2 * taps * BLOCK
    lanes = np.arange(width) % (taps * BLOCK) // 8
    return (np.arange(taps * C)[:, None] == lanes[None, :]).astype(ml_dtypes.bfloat16)


def offsets(taps):
    width = 2 * taps * BLOCK
    lanes = np.arange(width)
    place = lanes // (taps * BLOCK) * 8 + lanes % 8
    return (place[None, :] - np.arange(8)[:, None] - 4).astype(np.int32)


def split(value):
    high = value.astype(bf16)
    return high, (value - high.astype(f32)).astype(bf16)


def mul(a, b):
    return jnp.dot(a, b, preferred_element_type=f32)


def transform(planes, cols_ref, rows_ref, out_ref):
    lane = lax.broadcasted_iota(jnp.int32, (COLS, 256), 1)
    slot = (lane >> 5) & 3
    zero = jnp.zeros((), bf16)
    placed = [[jnp.where(slot == i, cols_ref[t], zero) for i in range(4)] for t in range(2)]
    rows_high, rows_low = rows_ref[0, 0], rows_ref[0, 1]
    for group in range(GROUPS):
        members = [planes(4 * group + i) for i in range(4)]
        sums = []
        for t in range(2):
            total = mul(members[0], placed[t][0])
            for i in range(1, 4):
                total = total + mul(members[i], placed[t][i])
            sums.append(total)
        high, low = split(jnp.concatenate(sums, axis=0))
        modes = mul(rows_high, high) + mul(rows_high, low) + mul(rows_low, high)
        for half in range(2):
            out_ref[pl.ds(half, 64, stride=2), group, :] = modes[:, 128 * half : 128 * half + 128]


def forward_kernel(place_ref, grid_ref, cols_ref, rows_ref, out_ref):
    transform(lambda c: grid_ref[c], cols_ref, rows_ref, out_ref)


def mix_kernel(mixture_ref, received_ref, weights_ref, out_ref, *, layer):
    total = jnp.sum(received_ref[...], axis=0)
    lane = lax.broadcasted_iota(jnp.int32, (8, 128), 1)
    sub = lax.broadcasted_iota(jnp.int32, (8, 128), 0)
    own = (lane >> 4) == sub
    parts = []
    for group in range(GROUPS):
        row = jnp.broadcast_to(total[group : group + 1, :], (8, 128))
        row = jnp.where(own, row, 0.0)
        for shift in (64, 32, 16):
            row = row + pltpu.roll(row, shift, 1)
        parts.append(row)
    spectrum = jnp.concatenate(parts, axis=0)
    rows = [jnp.sum(weights_ref[g] * spectrum, axis=0, keepdims=True) for g in range(GROUPS)]
    mixed = jnp.concatenate(rows, axis=0) * mixture_ref[layer, 0]
    out_ref[...] = jnp.broadcast_to(mixed[None], out_ref.shape)


def edge_kernel(grid_ref, top_ref, bottom_ref, left_ref, right_ref):
    pick = lax.broadcasted_iota(jnp.int32, (8, COLS), 1) - lax.broadcasted_iota(
        jnp.int32, (8, COLS), 0
    )
    one = jnp.ones((), f32)
    zero = jnp.zeros((), f32)
    first = jnp.where(pick == 0, one, zero).astype(bf16)
    last = jnp.where(pick == COLS - 8, one, zero).astype(bf16)
    rows = jnp.concatenate(
        [
            grid_ref[...].reshape(C * ROWS, COLS),
            top_ref[...].reshape(BLOCK, COLS),
            bottom_ref[...].reshape(BLOCK, COLS),
        ],
        axis=0,
    )
    dims = (((1,), (1,)), ((), ()))
    for pattern, ref in ((first, left_ref), (last, right_ref)):
        ref[...] = lax.dot_general(pattern, rows, dims, preferred_element_type=f32).astype(bf16)


def banded(weights_ref, spread_ref, offsets_ref, steps, width):
    offset = offsets_ref[...][None]
    total = jnp.zeros((C, 8, width), f32)
    for index, step in enumerate(steps):
        taps = mul(weights_ref[index], spread_ref[...])
        total = jnp.where(offset == step, taps[:, None, :], total)
    return total.reshape(BLOCK, width).astype(bf16)


def convolve(mixture_ref, field, bands, out_ref, stacks, layer, first, count, width):
    near_band, far_band = bands
    near_stack, far_stack = stacks

    def shift(index, carry):
        block = field(first + index)
        for position, step in enumerate((-1, 0, 1)):
            moved = block if step == 0 else pltpu.roll(block, (-step) % WIDE, 1)
            start = pl.multiple_of((index * 3 + position) * BLOCK, 16)
            near_stack[pl.ds(start, BLOCK), :] = moved[:, :width].astype(bf16)
        for position, step in enumerate((-4, -2, 0, 2, 4)):
            moved = block if step == 0 else pltpu.roll(block, (-step) % WIDE, 1)
            start = pl.multiple_of((index * 5 + position) * BLOCK, 16)
            far_stack[pl.ds(start, BLOCK), :] = moved[:, :width].astype(bf16)
        return carry

    lax.fori_loop(0, count + 1, shift, 0)
    near_scale = mixture_ref[layer, 1]
    far_scale = mixture_ref[layer, 2]

    def block_sum(index, carry):
        near_rows = near_stack[pl.ds(pl.multiple_of(index * 3 * BLOCK, 16), 6 * BLOCK), :]
        far_rows = far_stack[pl.ds(pl.multiple_of(index * 5 * BLOCK, 16), 10 * BLOCK), :]
        total = near_scale * mul(near_band[...], near_rows) + far_scale * mul(
            far_band[...], far_rows
        )
        out_ref[pl.ds(pl.multiple_of(index * BLOCK, 8), BLOCK), :] = total
        return carry

    lax.fori_loop(0, count, block_sum, 0)


def first_conv_kernel(
    mixture_ref, grid_ref, top_ref, bottom_ref, left_ref, right_ref, near_ref, far_ref,
    near_spread, far_spread, near_offsets, far_offsets, order_ref, out_ref,
    field, near_band, far_band, near_stack, far_stack, *, first, count,
):
    near_band[...] = banded(near_ref, near_spread, near_offsets, (-1, 0, 1), 6 * BLOCK)
    far_band[...] = banded(far_ref, far_spread, far_offsets, (-4, -2, 0, 2, 4), 10 * BLOCK)
    lane = lax.broadcasted_iota(jnp.int32, (8, 128), 1)
    row = lax.broadcasted_iota(jnp.int32, (8, 128), 0)
    right_place = jnp.where(lane == row, 1.0, 0.0).astype(bf16)
    left_place = jnp.where(lane == row + 120, 1.0, 0.0).astype(bf16)
    dims = (((0,), (0,)), ((), ()))
    side = lax.dot_general(
        right_ref[...], right_place, dims, preferred_element_type=f32
    ) + lax.dot_general(left_ref[...], left_place, dims, preferred_element_type=f32)
    for c in range(C):
        main = grid_ref[c].astype(f32)
        for block in range(first, first + count + 1):
            if block == 0:
                value = top_ref[c].astype(f32)
                edge = side[C * ROWS + 8 * c : C * ROWS + 8 * c + 8]
            elif block == 17:
                value = bottom_ref[c].astype(f32)
                edge = side[C * ROWS + BLOCK + 8 * c : C * ROWS + BLOCK + 8 * c + 8]
            else:
                start = 8 * (block - 1)
                value = main[start : start + 8]
                edge = side[c * ROWS + start : c * ROWS + start + 8]
            place = (block - first) * BLOCK + 8 * c
            field[place : place + 8, :COLS] = value
            field[place : place + 8, COLS:] = edge
    def part(index):
        return field[pl.ds(pl.multiple_of((index - first) * BLOCK, 8), BLOCK), :]

    convolve(
        mixture_ref, part, (near_band, far_band), out_ref, (near_stack, far_stack), 0, first,
        count, WIDE,
    )


def second_conv_kernel(
    mixture_ref, field_ref, near_ref, far_ref, near_spread, far_spread, near_offsets,
    far_offsets, order_ref, out_ref, near_band, far_band, near_stack, far_stack, *, first, count,
):
    near_band[...] = banded(near_ref, near_spread, near_offsets, (-1, 0, 1), 6 * BLOCK)
    far_band[...] = banded(far_ref, far_spread, far_offsets, (-4, -2, 0, 2, 4), 10 * BLOCK)

    def part(index):
        return field_ref[pl.ds(pl.multiple_of(index * BLOCK, 8), BLOCK), :]

    convolve(
        mixture_ref, part, (near_band, far_band), out_ref, (near_stack, far_stack), 1, first,
        count, COLS,
    )


def gelu(value):
    return 0.5 * value * (1.0 + lax.erf(value * math.sqrt(0.5)))


def expand(bias_ref, gathered_ref, cols_ref, rows_ref, upper_ref, lower_ref, layer, width, blocks, emit):
    parts = []
    for group in range(GROUPS):
        pair = [gathered_ref[pl.ds(half, 64, stride=2), group, :] for half in range(2)]
        parts.append(jnp.concatenate(pair, axis=1))
    high, low = split(jnp.concatenate(parts, axis=0))
    stacked = jnp.concatenate([high, low], axis=0)
    rows_high, rows_low = rows_ref[0, 0], rows_ref[0, 1]
    rows_twice = jnp.concatenate([rows_high, rows_high], axis=1)
    upper_blocks = upper_ref.shape[0] // BLOCK
    for slot in range(4):
        placed = []
        for t in range(2):
            table = cols_ref[0, t]
            empty = jnp.zeros((32, 2 * width), bf16)
            pieces = []
            for half in range(2):
                pieces += [table[32 * half : 32 * half + 32] if i == slot else empty for i in range(4)]
            placed.append(jnp.concatenate(pieces, axis=0))
        first = mul(stacked, placed[0])
        lines = first[:320] + first[320:] + mul(high, placed[1])
        for group in range(GROUPS):
            channel = 4 * group + slot
            here = lines[64 * group : 64 * group + 64]
            line_high, line_low = split(jnp.concatenate([here[:, :width], here[:, width:]], axis=0))
            value = mul(rows_twice, jnp.concatenate([line_high, line_low], axis=0)) + mul(
                rows_low, line_high
            )
            local = []
            for block in range(blocks):
                ref, index = (
                    (upper_ref, block) if block < upper_blocks else (lower_ref, block - upper_blocks)
                )
                local.append(ref[index * BLOCK + 8 * channel : index * BLOCK + 8 * channel + 8, :])
            value = value + jnp.concatenate(local, axis=0) + bias_ref[layer, channel]
            emit(channel, gelu(value))


def middle_kernel(
    place_ref, bias_ref, gathered_ref, icols_ref, irows_ref, fcols_ref, frows_ref, upper_ref,
    lower_ref, field_ref, out_ref, planes,
):
    def emit(channel, value):
        rounded = value.astype(bf16)
        planes[channel, :136] = rounded[:, :COLS]
        planes[channel, 136:] = jnp.zeros((8, COLS), bf16)
        back = rounded.astype(f32)
        for block in range(17):
            place = block * BLOCK + 8 * channel
            field_ref[place : place + 8, :] = back[8 * block : 8 * block + 8]

    expand(bias_ref, gathered_ref, icols_ref, irows_ref, upper_ref, lower_ref, 0, WIDE, 17, emit)
    transform(lambda c: planes[c], fcols_ref, frows_ref, out_ref)


def last_kernel(
    place_ref, bias_ref, gathered_ref, icols_ref, irows_ref, upper_ref, lower_ref, out_ref
):
    def emit(channel, value):
        out_ref[channel] = value.astype(bf16)

    expand(bias_ref, gathered_ref, icols_ref, irows_ref, upper_ref, lower_ref, 1, COLS, 16, emit)


vmem = pl.BlockSpec(memory_space=pltpu.VMEM)
smem = pl.BlockSpec(memory_space=pltpu.SMEM)
anywhere = pl.BlockSpec(memory_space=pl.ANY)
limit = pltpu.CompilerParams(vmem_limit_bytes=56 * 1024 * 1024)


def call(kernel, outs, args, specs, scratch=(), flops=10**9, name=None):
    single = not isinstance(outs, (list, tuple))
    return pl.pallas_call(
        kernel,
        out_shape=outs,
        in_specs=specs,
        out_specs=vmem if single else [vmem] * len(outs),
        scratch_shapes=list(scratch),
        compiler_params=limit,
        cost_estimate=pl.CostEstimate(flops=flops, bytes_accessed=4 * 10**6, transcendentals=0),
        name=name,
    )(*args)


def whole(shape):
    zeros = (0,) * len(shape)
    return pl.BlockSpec(shape, lambda i, place: zeros)


def chosen(shape, axis, dim=0):
    def index(i, place):
        return tuple(place[axis] if d == dim else 0 for d in range(len(shape)))

    return pl.BlockSpec(shape, index)


def placed_call(kernel, outs, place, args, specs, scratch=(), flops=10**9, name=None):
    single = not isinstance(outs, (list, tuple))
    shapes = [outs] if single else list(outs)
    out_specs = [whole(s.shape) for s in shapes]
    return pl.pallas_call(
        kernel,
        out_shape=outs,
        grid_spec=pltpu.PrefetchScalarGridSpec(
            num_scalar_prefetch=1,
            grid=(1,),
            in_specs=specs,
            out_specs=out_specs[0] if single else out_specs,
            scratch_shapes=list(scratch),
        ),
        compiler_params=limit,
        cost_estimate=pl.CostEstimate(flops=flops, bytes_accessed=4 * 10**6, transcendentals=0),
        name=name,
    )(place, *args)


def shape_of(dims, kind):
    return jax.ShapeDtypeStruct(dims, kind)


def exchange(value):
    return lax.all_to_all(value, both, split_axis=0, concat_axis=0, tiled=True)


def ring(axis, step):
    size = lax.axis_size(axis)
    return [(i, (i + step) % size) for i in range(size)]


def on_device(grid_field, spectral_weight, conv_near, conv_far, mix_logits, channel_bias):
    place = jnp.stack([lax.axis_index("gx"), lax.axis_index("gy")]).astype(jnp.int32)
    grid = grid_field[0]
    top = lax.ppermute(grid[:, ROWS - 8 :], "gx", ring("gx", 1))
    bottom = lax.ppermute(grid[:, :8], "gx", ring("gx", -1))

    exponents = jnp.exp(mix_logits)
    mixture = exponents / jnp.sum(exponents, axis=1, keepdims=True)
    near = jnp.transpose(conv_near.reshape(LAYERS, C, 3, 3 * C), (0, 2, 1, 3))
    far = jnp.transpose(conv_far.reshape(LAYERS, C, 5, 5 * C), (0, 2, 1, 3))
    real, imaginary = spectral_weight[:, 0], spectral_weight[:, 1]
    from_real = jnp.stack([real, imaginary], axis=3)
    from_imaginary = jnp.stack([-imaginary, real], axis=3)
    weights = jnp.stack([from_real, from_imaginary], axis=2)
    weights = weights.reshape(LAYERS, 2 * C, GROUPS, 128)
    weights = jnp.transpose(weights, (0, 2, 1, 3))

    fcols = jnp.asarray(forward_cols())
    frows = jnp.asarray(forward_rows(0, ROWS))
    frows_wide = jnp.asarray(forward_rows(4, 144))
    irows = jnp.asarray(inverse_rows(0, ROWS))
    irows_wide = jnp.asarray(inverse_rows(4, 136))
    icols = jnp.asarray(inverse_cols(COLS))
    icols_wide = jnp.asarray(inverse_cols(WIDE))
    tables = [jnp.asarray(t) for t in (spread(3), spread(5), offsets(3), offsets(5))]

    fcols_spec = chosen((2, COLS, 256), 1, 1)
    chunk = shape_of((128, GROUPS, 128), f32)

    partial = placed_call(
        forward_kernel, chunk, place, (grid, fcols, frows),
        [whole((C, ROWS, COLS)), fcols_spec, chosen((1, 2, 64, 2 * ROWS), 0)],
        name="forward",
    )
    received = exchange(partial)
    first_cols, last_cols = call(
        edge_kernel, [shape_of((8, 18 * BLOCK), bf16)] * 2, (grid, top, bottom), [vmem] * 3,
        name="edges",
    )
    left = lax.ppermute(last_cols, "gy", ring("gy", 1))
    right = lax.ppermute(first_cols, "gy", ring("gy", -1))

    def mix(layer, received):
        return call(
            functools.partial(mix_kernel, layer=layer), chunk, (mixture, received, weights[layer]),
            [smem, vmem, vmem], flops=10**6, name="mix",
        )

    def stacks(count, width):
        return (
            pltpu.VMEM((BLOCK, 6 * BLOCK), bf16),
            pltpu.VMEM((BLOCK, 10 * BLOCK), bf16),
            pltpu.VMEM(((count + 1) * 3 * BLOCK, width), bf16),
            pltpu.VMEM(((count + 1) * 5 * BLOCK, width), bf16),
        )

    def first_conv(first, count, order):
        return call(
            functools.partial(first_conv_kernel, first=first, count=count),
            shape_of((count * BLOCK, WIDE), f32),
            (mixture, grid, top, bottom, left, right, near[0], far[0], *tables, order),
            [smem] + [vmem] * 11 + [anywhere],
            (pltpu.VMEM(((count + 1) * BLOCK, WIDE), f32), *stacks(count, WIDE)),
            name="conv_first",
        )

    def second_conv(field, first, count, order):
        return call(
            functools.partial(second_conv_kernel, first=first, count=count),
            shape_of((count * BLOCK, COLS), f32),
            (mixture, field, near[1], far[1], *tables, order),
            [smem] + [vmem] * 7 + [anywhere],
            stacks(count, COLS),
            name="conv_second",
        )

    upper = first_conv(0, 9, place)
    mixed = mix(0, received)
    gathered = exchange(mixed)
    lower = first_conv(9, 8, mixed)
    field, partial = placed_call(
        middle_kernel, [shape_of((17 * BLOCK, WIDE), f32), chunk], place,
        (channel_bias, gathered, icols_wide, irows_wide, fcols, frows_wide, upper, lower),
        [
            smem, whole((128, GROUPS, 128)), chosen((1, 2, 64, 2 * WIDE), 1),
            chosen((1, 2, 136, 128), 0), fcols_spec, chosen((1, 2, 64, 288), 0),
            whole((9 * BLOCK, WIDE)), whole((8 * BLOCK, WIDE)),
        ],
        (pltpu.VMEM((C, 144, COLS), bf16),),
        name="middle",
    )
    received = exchange(partial)
    upper = second_conv(field, 0, 8, place)
    mixed = mix(1, received)
    gathered = exchange(mixed)
    lower = second_conv(field, 8, 8, mixed)
    result = placed_call(
        last_kernel, shape_of((C, ROWS, COLS), bf16), place,
        (channel_bias, gathered, icols, irows, upper, lower),
        [
            smem, whole((128, GROUPS, 128)), chosen((1, 2, 64, 2 * COLS), 1),
            chosen((1, 2, ROWS, 128), 0), whole((8 * BLOCK, COLS)), whole((8 * BLOCK, COLS)),
        ],
        name="last",
    )
    return result[None]


def solution(mesh):
    in_specs = (
        P(None, None, "gx", "gy"),
        P(None, None, None, None, both),
        P(),
        P(),
        P(),
        P(),
    )
    out_specs = P(None, None, "gx", "gy")
    return jax.shard_map(
        on_device, mesh=mesh, in_specs=in_specs, out_specs=out_specs, check_vma=False
    )
```

```python
import functools
import math

import jax
import jax.numpy as jnp
import ml_dtypes
import numpy as np
from jax import lax
from jax.experimental import pallas as pl
from jax.experimental.pallas import tpu as pltpu
from jax.sharding import PartitionSpec as P

NX = 2048
NY = 2048
C = 20
LAYERS = 2
ROWS = 128
COLS = 256
GROUPS = 5
WIDE = 384
BLOCK = 8 * C

f32 = jnp.float32
bf16 = jnp.bfloat16
both = ("gx", "gy")
WIRES = (jnp.float32, jnp.bfloat16)


def wave(numbers, positions, length):
    product = numbers.astype(np.int64)[:, None] * positions.astype(np.int64)[None, :]
    scale = np.float32(2.0 * math.pi / length)
    angle = (product % length).astype(np.float32) * scale
    angle = angle.astype(np.float64)
    return np.cos(angle).astype(np.float32), np.sin(angle).astype(np.float32)


def halves(value):
    high = value.astype(ml_dtypes.bfloat16)
    low = (value - high.astype(np.float32)).astype(ml_dtypes.bfloat16)
    return high, low


ky_all = np.arange(32)
kx_all = np.concatenate([np.arange(32), np.arange(32) + NX - 32])


def forward_cols():
    cosine, sine = wave(ky_all, np.arange(NY), NY)
    cosine, sine = cosine.T.reshape(NY, 2, 1, 16), sine.T.reshape(NY, 2, 1, 16)
    first = np.stack([cosine, -sine], axis=3)
    second = np.stack([-sine, -cosine], axis=3)
    tables = [np.broadcast_to(t, (NY, 2, 4, 2, 16)).reshape(NY, 256) for t in (first, second)]
    return np.stack(tables).astype(ml_dtypes.bfloat16)


def forward_rows(before, count):
    out = np.zeros((16, 2, 64, 2 * count), ml_dtypes.bfloat16)
    for device in range(16):
        cosine, sine = wave(kx_all, np.arange(ROWS) + device * ROWS, NX)
        table = np.zeros((2, 64, count), np.float32)
        table[0, :, before : before + ROWS] = cosine
        table[1, :, before : before + ROWS] = sine
        high, low = halves(np.transpose(table, (1, 0, 2)).reshape(64, 2 * count))
        out[device, 0], out[device, 1] = high, low
    return out


def inverse_rows(before, count):
    out = np.zeros((16, 2, count, 128), ml_dtypes.bfloat16)
    for device in range(16):
        positions = (np.arange(count) - before + device * ROWS) % NX
        cosine, sine = wave(kx_all, positions, NX)
        high, low = halves(np.concatenate([cosine.T, -sine.T], axis=1))
        out[device, 0], out[device, 1] = high, low
    return out


def inverse_cols():
    width = COLS
    out = np.zeros((8, 2, 64, 2 * width), ml_dtypes.bfloat16)
    weight = (np.where(ky_all == 0, 1.0, 2.0) / (NX * NY)).astype(np.float32)[:, None]
    for device in range(8):
        cosine, sine = wave(ky_all, np.arange(width) + device * COLS, NY)
        cosine, sine = cosine * weight, sine * weight
        real = np.concatenate([cosine, sine], axis=1)
        imaginary = np.concatenate([-sine, cosine], axis=1)
        table = np.stack([real.reshape(2, 16, 2 * width), imaginary.reshape(2, 16, 2 * width)], 1)
        high, low = halves(table.reshape(64, 2 * width))
        out[device, 0], out[device, 1] = high, low
    return out


def spread(taps, slots_first):
    width = 2 * taps * BLOCK
    lanes = np.arange(width) % (taps * BLOCK) // 8
    step, channel = lanes // C, lanes % C
    if slots_first:
        channel = channel % GROUPS * 4 + channel // GROUPS
    columns = step * C + channel
    return (np.arange(taps * C)[:, None] == columns[None, :]).astype(ml_dtypes.bfloat16)


def offsets(taps):
    width = 2 * taps * BLOCK
    lanes = np.arange(width)
    place = lanes // (taps * BLOCK) * 8 + lanes % 8
    return (place[None, :] - np.arange(8)[:, None] - 4).astype(np.int32)


def split(value):
    high = value.astype(bf16)
    return high, (value - high.astype(f32)).astype(bf16)


def mul(a, b):
    return jnp.dot(a, b, preferred_element_type=f32)


def fetch(pairs):
    copies = [pltpu.make_async_copy(source, target, sem) for source, target, sem in pairs]
    for copy in copies:
        copy.start()
    return copies


def transform(planes, cols_ref, rows_ref, write):
    lane = lax.broadcasted_iota(jnp.int32, (COLS, 256), 1)
    slot = (lane >> 5) & 3
    zero = jnp.zeros((), bf16)
    placed = [[jnp.where(slot == i, cols_ref[t], zero) for i in range(4)] for t in range(2)]
    rows_high, rows_low = rows_ref[0], rows_ref[1]
    for group in range(GROUPS):
        members = [planes(4 * group + i) for i in range(4)]
        sums = []
        for t in range(2):
            total = mul(members[0], placed[t][0])
            for i in range(1, 4):
                total = total + mul(members[i], placed[t][i])
            sums.append(total)
        high, low = split(jnp.concatenate(sums, axis=0))
        modes = mul(rows_high, high) + mul(rows_high, low) + mul(rows_low, high)
        for half in range(2):
            write(half, group, modes[:, 128 * half : 128 * half + 128])


def indices():
    return lax.axis_index("gx"), lax.axis_index("gy")


def forward_kernel(
    grid_all, cols_all, rows_all, out_ref, first_ref, last_ref, grid_buffer, cols, rows, sems
):
    gx, gy = indices()
    start = pl.multiple_of(gy * COLS, COLS)
    copies = fetch(
        [
            (cols_all.at[:, pl.ds(start, COLS), :], cols, sems.at[0]),
            (rows_all.at[0, gx, :, :, pl.ds(0, 2 * ROWS)], rows, sems.at[1]),
        ]
        + [
            (grid_all.at[pl.ds(4 * g, 4)], grid_buffer.at[pl.ds(4 * g, 4)], sems.at[2 + g])
            for g in range(GROUPS)
        ]
    )
    copies[0].wait()
    copies[1].wait()

    def plane(c):
        if c % 4 == 0:
            copies[2 + c // 4].wait()
        return grid_buffer[c]

    def write(half, group, value):
        out_ref[pl.ds(half, 64, stride=2), group, :] = value

    transform(plane, cols, rows, write)
    edges(grid_buffer[...].reshape(C * ROWS, COLS), first_ref, last_ref)


def mixture_of(logits_ref, layer):
    exponents = jnp.exp(logits_ref[layer : layer + 1, :])
    weights = exponents / jnp.sum(exponents, axis=1, keepdims=True)
    return [weights[:, i : i + 1] for i in range(3)]


def mix_kernel(logits_ref, received_ref, weights_all, order_ref, out_ref, marker_ref, weights_ref, sem, *, layer):
    (copy,) = fetch([(weights_all.at[layer], weights_ref, sem)])
    total = jnp.sum(received_ref[...].astype(f32), axis=0)
    total = jnp.concatenate([total, jnp.zeros((8 - GROUPS, 128), f32)], axis=0)
    columns = jnp.transpose(total)
    real = jnp.zeros((16, C), f32)
    imaginary = jnp.zeros((16, C), f32)
    copy.wait()
    for c in range(C):
        group, start = c // 4, c % 4 * 32
        in_real = columns[start : start + 16, group : group + 1]
        in_imaginary = columns[start + 16 : start + 32, group : group + 1]
        weight_real, weight_imaginary = weights_ref[0, c], weights_ref[1, c]
        real = real + weight_real * in_real - weight_imaginary * in_imaginary
        imaginary = imaginary + weight_real * in_imaginary + weight_imaginary * in_real
    scale = mixture_of(logits_ref, layer)[0]
    lines = jnp.transpose(jnp.concatenate([real * scale, imaginary * scale] * 4, axis=0))
    lane = lax.broadcasted_iota(jnp.int32, (C, 128), 1)
    row = lax.broadcasted_iota(jnp.int32, (C, 128), 0)
    lines = jnp.where((lane >> 5) == (row & 3), lines, 0.0)
    group = lax.broadcasted_iota(jnp.int32, (8, C), 0)
    member = lax.broadcasted_iota(jnp.int32, (8, C), 1)
    gather = jnp.where((member >> 2) == group, 1.0, 0.0)
    mixed = jnp.dot(gather, lines, precision=lax.Precision.HIGHEST, preferred_element_type=f32)
    mixed = mixed[:GROUPS].astype(out_ref.dtype)
    out_ref[...] = jnp.broadcast_to(mixed[None], out_ref.shape)
    marker_ref[...] = lines[:8]


def edge_patterns():
    pick = lax.broadcasted_iota(jnp.int32, (8, COLS), 1) - lax.broadcasted_iota(
        jnp.int32, (8, COLS), 0
    )
    first = jnp.where(pick == 0, 1.0, 0.0).astype(bf16)
    last = jnp.where(pick == COLS - 8, 1.0, 0.0).astype(bf16)
    return first, last


def edge_columns(rows):
    dims = (((1,), (1,)), ((), ()))
    return [
        lax.dot_general(pattern, rows, dims, preferred_element_type=f32).astype(bf16)
        for pattern in edge_patterns()
    ]


def edges(rows, first_ref, last_ref):
    first_ref[...], last_ref[...] = edge_columns(rows)


def edges_kernel(top_ref, bottom_ref, first_ref, last_ref, first_out, last_out):
    rows = [r[...].reshape(BLOCK, COLS) for r in (top_ref, bottom_ref)]
    found = edge_columns(jnp.concatenate(rows, axis=0))
    for own_ref, extra, out_ref in zip((first_ref, last_ref), found, (first_out, last_out)):
        out_ref[:, : C * ROWS] = own_ref[...]
        out_ref[:, C * ROWS :] = extra


def banded(weights, spread_ref, offsets_ref, steps, width):
    offset = offsets_ref[...][None]
    total = jnp.zeros((C, 8, width), f32)
    taps = len(steps) * C
    for index, step in enumerate(steps):
        own = mul(weights[:, taps * index : taps * index + taps], spread_ref[...])
        total = jnp.where(offset == step, own[:, None, :], total)
    return total.reshape(BLOCK, width).astype(bf16)


NEAR = (-1, 0, 1)
FAR = (-4, -2, 0, 2, 4)


def conv_kernel(logits_ref, *refs, layer, count):
    sources, refs = (refs[:3], refs[3:]) if layer == 0 else (refs[:1], refs[1:])
    left_ref, right_ref, near_ref, far_ref, refs = *refs[:4], refs[4:]
    near_spread, far_spread, near_offsets, far_offsets, order_ref, out_all, marker_ref, *refs = refs
    field, out_ref, near_band, far_band, near_stack, far_stack, *refs = refs
    sems, out_sems, *refs = refs
    if layer == 0:
        grid_all, top_ref, bottom_ref = sources
        (grid_ref,) = refs
        copies = fetch(
            [
                (grid_all.at[pl.ds(4 * g, 4)], grid_ref.at[pl.ds(4 * g, 4)], sems.at[g])
                for g in range(GROUPS)
            ]
        )
    else:
        (field_all,) = sources
        pieces = [pl.ds(i * BLOCK, min(3, count + 1 - i) * BLOCK) for i in range(0, count + 1, 3)]
        copies = fetch(
            [(field_all.at[p], field.at[p], sems.at[k]) for k, p in enumerate(pieces)]
        )
    near_band[...] = banded(near_ref[layer], near_spread, near_offsets, NEAR, 6 * BLOCK)
    far_band[...] = banded(far_ref[layer], far_spread, far_offsets, FAR, 10 * BLOCK)
    lane = lax.broadcasted_iota(jnp.int32, (16, 128), 1)
    row = lax.broadcasted_iota(jnp.int32, (16, 128), 0)
    sides_place = jnp.where(lane == jnp.where(row < 8, row, row + 112), 1.0, 0.0).astype(bf16)
    sides = jnp.concatenate([right_ref[...].astype(f32), left_ref[...].astype(f32)], axis=0)
    side = lax.dot_general(
        sides.astype(bf16), sides_place, (((0,), (0,)), ((), ())), preferred_element_type=f32
    )
    if layer == 0:
        for pair in range(C // 2):
            if pair % 2 == 0:
                copies[pair // 2].wait()
            inner = [grid_ref[2 * pair + i].astype(f32) for i in range(2)]
            upper = [top_ref[2 * pair + i].astype(f32) for i in range(2)]
            lower = [bottom_ref[2 * pair + i].astype(f32) for i in range(2)]
            for block in range(18):
                if block == 0:
                    value = upper
                elif block == 17:
                    value = lower
                else:
                    value = [v[8 * block - 8 : 8 * block] for v in inner]
                place = block * BLOCK + 16 * pair
                field[place : place + 16, :] = jnp.concatenate(value, axis=0).astype(bf16)

    def side_of(block):
        if layer == 1 or block in (0, 17):
            start = block * BLOCK if layer == 1 else C * ROWS + (block > 0) * BLOCK
            return side[start : start + BLOCK].astype(bf16)
        starts = [c * ROWS + 8 * block - 8 for c in range(C)]
        return jnp.concatenate([side[p : p + 8] for p in starts], axis=0).astype(bf16)

    _, near_scale, far_scale = mixture_of(logits_ref, layer)
    results = []
    for index in range(count + 1):
        if layer == 1 and index % 3 == 0:
            copies[index // 3].wait()
        rows = slice(index * BLOCK, index * BLOCK + BLOCK)
        block = jnp.concatenate([field[rows, :], side_of(index)], axis=1)
        moved = {0: block}
        for step in (-4, -2, -1, 1, 2, 4):
            moved[step] = pltpu.roll(block, (-step) % WIDE, 1)
        for steps, stack in ((NEAR, near_stack), (FAR, far_stack)):
            for position, step in enumerate(steps):
                start = (index * len(steps) + position) * BLOCK
                stack[start : start + BLOCK, :] = moved[step][:, :COLS]
        if index == 0:
            continue
        done = index - 1
        near_rows = near_stack[done * 3 * BLOCK : (done + 2) * 3 * BLOCK, :]
        far_rows = far_stack[done * 5 * BLOCK : (done + 2) * 5 * BLOCK, :]
        total = near_scale * mul(near_band[...], near_rows) + far_scale * mul(
            far_band[...], far_rows
        )
        out_ref[done * BLOCK : done * BLOCK + BLOCK, :] = total
        piece = pl.ds(done * BLOCK, BLOCK)
        results += fetch([(out_ref.at[piece], out_all.at[piece], out_sems.at[done])])
    marker_ref[...] = total[:8, :128]
    for copy in results:
        copy.wait()


def gelu(value):
    return 0.5 * value * (1.0 + lax.erf(value * math.sqrt(0.5)))


def expand(bias_ref, gathered, cols, rows, conv_ref, conv_copy, layer, blocks, emit):
    parts = []
    for group in range(GROUPS):
        pair = [gathered[pl.ds(half, 64, stride=2), group, :] for half in range(2)]
        parts.append(jnp.concatenate(pair, axis=1))
    high, low = split(jnp.concatenate(parts, axis=0))
    stacked = jnp.concatenate([high, low], axis=0)
    rows_high, rows_low = rows[0], rows[1]
    rows_twice = jnp.concatenate([rows_high, rows_high], axis=1)
    empty = jnp.zeros((32, 2 * COLS), bf16)
    for slot in range(4):
        placed = []
        for t in range(2):
            table = cols[t]
            pieces = []
            for half in range(2):
                own = table[32 * half : 32 * half + 32]
                pieces += [own if i == slot else empty for i in range(4)]
            placed.append(jnp.concatenate(pieces, axis=0))
        first = mul(stacked, placed[0])
        lines = first[:320] + first[320:] + mul(high, placed[1])
        if slot == 0:
            conv_copy.wait()
        for group in range(GROUPS):
            channel = 4 * group + slot
            here = lines[64 * group : 64 * group + 64]
            line_high, line_low = split(jnp.concatenate([here[:, :COLS], here[:, COLS:]], axis=0))
            value = mul(rows_twice, jnp.concatenate([line_high, line_low], axis=0)) + mul(
                rows_low, line_high
            )
            local = []
            for block in range(blocks):
                place = block * BLOCK + 8 * channel
                local.append(conv_ref[place : place + 8, :])
            value = value + jnp.concatenate(local, axis=0) + bias_ref[layer, channel]
            emit(slot * GROUPS + group, channel, gelu(value))


def middle_kernel(
    bias_ref, gathered_ref, icols_all, irows_all, fcols_all, frows_all, conv_all,
    field_all, first_ref, last_ref, out_ref,
    planes, chunk, icols, irows, fcols, frows, conv_ref, field_ref, sems,
):
    gx, gy = indices()
    start = pl.multiple_of(gy * COLS, COLS)
    copies = fetch(
        [
            (icols_all.at[0, gy], icols, sems.at[0]),
            (irows_all.at[1, gx], irows, sems.at[1]),
            (fcols_all.at[:, pl.ds(start, COLS), :], fcols, sems.at[2]),
            (conv_all, conv_ref, sems.at[4]),
            (frows_all.at[1, gx], frows, sems.at[3]),
        ]
    )
    copies[0].wait()
    copies[1].wait()
    waiting = []

    def emit(order, channel, value):
        rounded = value.astype(bf16)
        planes[channel, :136] = rounded
        planes[channel, 136:] = jnp.zeros((8, COLS), bf16)
        waiting.append(rounded.astype(f32))
        if order % 2 == 1:
            for block in range(17):
                rows = slice(8 * block, 8 * block + 8)
                both_rows = jnp.concatenate([waiting[0][rows], waiting[1][rows]], axis=0)
                place = block * BLOCK + 8 * (order - 1)
                field_ref[place : place + 16, :] = both_rows.astype(bf16)
            waiting.clear()

    expand(bias_ref, gathered_ref, icols, irows, conv_ref, copies[3], 0, 17, emit)
    (result,) = fetch([(field_ref, field_all, sems.at[5])])
    edges(field_ref[...], first_ref, last_ref)
    copies[2].wait()
    copies[4].wait()

    def write(half, group, value):
        chunk[pl.ds(half, 64, stride=2), group, :] = value

    transform(lambda c: planes[c], fcols, frows, write)
    out_ref[...] = chunk[...].astype(out_ref.dtype)
    result.wait()


def last_kernel(
    bias_ref, gathered_ref, icols_all, irows_all, conv_all, out_all,
    wide, icols, irows, conv_ref, out_ref, sems, out_sems,
):
    gx, gy = indices()
    copies = fetch(
        [
            (icols_all.at[0, gy], icols, sems.at[0]),
            (irows_all.at[0, gx, :, pl.ds(0, ROWS)], irows, sems.at[1]),
            (conv_all, conv_ref, sems.at[2]),
        ]
    )
    wide[...] = gathered_ref[...].astype(f32)
    copies[0].wait()
    copies[1].wait()
    results = []

    def emit(order, channel, value):
        out_ref[channel] = value.astype(bf16)
        results.extend(fetch([(out_ref.at[channel], out_all.at[channel], out_sems.at[channel])]))

    expand(bias_ref, wide, icols, irows, conv_ref, copies[2], 1, 16, emit)
    for copy in results:
        copy.wait()


vmem = pl.BlockSpec(memory_space=pltpu.VMEM)
smem = pl.BlockSpec(memory_space=pltpu.SMEM)
anywhere = pl.BlockSpec(memory_space=pl.ANY)
hbm = pl.BlockSpec(memory_space=pltpu.HBM)
LIMIT = 56 * 10**6
SMALL = 4 * 10**6


def call(kernel, outs, args, specs, scratch=(), out_specs=None, flops=10**9, limit=LIMIT, name=None):
    single = not isinstance(outs, (list, tuple))
    if out_specs is None:
        out_specs = vmem if single else [vmem] * len(outs)
    return pl.pallas_call(
        kernel,
        out_shape=outs,
        in_specs=specs,
        out_specs=out_specs,
        scratch_shapes=list(scratch),
        compiler_params=pltpu.CompilerParams(vmem_limit_bytes=limit),
        cost_estimate=pl.CostEstimate(flops=flops, bytes_accessed=4 * 10**6, transcendentals=0),
        name=name,
    )(*args)


def shape_of(dims, kind):
    return jax.ShapeDtypeStruct(dims, kind)


def exchange(value):
    return lax.all_to_all(value, both, split_axis=0, concat_axis=0, tiled=True)


def ring(axis, step):
    size = lax.axis_size(axis)
    return [(i, (i + step) % size) for i in range(size)]


def sides(first, last):
    left = lax.ppermute(last, "gy", ring("gy", 1))
    right = lax.ppermute(first, "gy", ring("gy", -1))
    return left, right


def on_device(grid_field, spectral_weight, conv_near, conv_far, mix_logits, channel_bias):
    grid = grid_field[0]
    top = lax.ppermute(grid[:, ROWS - 8 :], "gx", ring("gx", 1))
    bottom = lax.ppermute(grid[:, :8], "gx", ring("gx", -1))
    mode_weights = jnp.swapaxes(spectral_weight, 3, 4)

    fcols = jnp.asarray(forward_cols())
    plain, wide = forward_rows(0, ROWS), forward_rows(4, 144)
    frows = np.zeros((2,) + wide.shape, wide.dtype)
    frows[0, ..., : 2 * ROWS], frows[1] = plain, wide
    plain, wide = inverse_rows(0, ROWS), inverse_rows(4, 136)
    irows = np.zeros((2,) + wide.shape, wide.dtype)
    irows[0, :, :, :ROWS], irows[1] = plain, wide
    icols = np.stack([inverse_cols()] * 2)
    frows, irows, icols = jnp.asarray(frows), jnp.asarray(irows), jnp.asarray(icols)

    chunks = [shape_of((128, GROUPS, 128), kind) for kind in WIRES]
    dma = pltpu.SemaphoreType.DMA
    icols_buffer = pltpu.VMEM((2, 64, 2 * COLS), bf16)
    fcols_buffer = pltpu.VMEM((2, COLS, 256), bf16)

    partial, first, last = call(
        forward_kernel, [chunks[0]] + [shape_of((8, C * ROWS), bf16)] * 2, (grid, fcols, frows),
        [hbm] * 3,
        (
            pltpu.VMEM((C, ROWS, COLS), bf16), fcols_buffer, pltpu.VMEM((2, 64, 2 * ROWS), bf16),
            dma((2 + GROUPS,)),
        ),
        name="forward",
    )
    received = exchange(partial)
    first, last = call(
        edges_kernel, [shape_of((8, 18 * BLOCK), bf16)] * 2, (top, bottom, first, last),
        [vmem] * 4, limit=SMALL, name="edges",
    )

    def mix(layer, received, order):
        return call(
            functools.partial(mix_kernel, layer=layer), [chunks[layer], shape_of((8, 128), f32)],
            (mix_logits, received, mode_weights, order), [vmem, vmem, hbm, anywhere],
            (pltpu.VMEM((2, C, 16, C), f32), dma), flops=10**6, limit=SMALL, name="mix",
        )

    def conv(layer, sources, specs, sides, count, order):
        tables = (spread(3, layer), spread(5, layer), offsets(3), offsets(5))
        return call(
            functools.partial(conv_kernel, layer=layer, count=count),
            [shape_of((count * BLOCK, COLS), f32), shape_of((8, 128), f32)],
            (mix_logits, *sources, *sides, conv_near, conv_far, *map(jnp.asarray, tables), order),
            [vmem] + specs + [vmem] * 8 + [anywhere],
            [
                pltpu.VMEM(((count + 1) * BLOCK, COLS), bf16),
                pltpu.VMEM((count * BLOCK, COLS), f32),
                pltpu.VMEM((BLOCK, 6 * BLOCK), bf16),
                pltpu.VMEM((BLOCK, 10 * BLOCK), bf16),
                pltpu.VMEM(((count + 1) * 3 * BLOCK, COLS), bf16),
                pltpu.VMEM(((count + 1) * 5 * BLOCK, COLS), bf16),
                dma((6,)), dma((count,)),
            ]
            + [pltpu.VMEM((C, ROWS, COLS), bf16)] * (1 - layer),
            out_specs=[hbm, vmem], flops=2 * 10**10, name="conv",
        )

    around = sides(first, last)
    mixed, marker = mix(0, received, mix_logits)
    gathered = exchange(mixed)
    local, _ = conv(0, (grid, top, bottom), [hbm, vmem, vmem], around, 17, marker)
    field, first, last, partial = call(
        middle_kernel,
        [shape_of((17 * BLOCK, COLS), bf16)] + [shape_of((8, 17 * BLOCK), bf16)] * 2 + [chunks[1]],
        (channel_bias, gathered, icols, irows, fcols, frows, local),
        [smem, vmem] + [hbm] * 5,
        (
            pltpu.VMEM((C, 144, COLS), bf16), pltpu.VMEM((128, GROUPS, 128), f32),
            icols_buffer, pltpu.VMEM((2, 136, 128), bf16),
            fcols_buffer, pltpu.VMEM((2, 64, 288), bf16),
            pltpu.VMEM((17 * BLOCK, COLS), f32), pltpu.VMEM((17 * BLOCK, COLS), bf16), dma((6,)),
        ),
        out_specs=[hbm, vmem, vmem, vmem],
        name="middle",
    )
    received = exchange(partial)
    local, marker = conv(1, (field,), [hbm], sides(first, last), 16, mix_logits)
    mixed, _ = mix(1, received, marker)
    gathered = exchange(mixed)
    result = call(
        last_kernel, shape_of((C, ROWS, COLS), bf16),
        (channel_bias, gathered, icols, irows, local),
        [smem, vmem] + [hbm] * 3,
        (
            pltpu.VMEM((128, GROUPS, 128), f32), icols_buffer, pltpu.VMEM((2, ROWS, 128), bf16),
            pltpu.VMEM((16 * BLOCK, COLS), f32), pltpu.VMEM((C, ROWS, COLS), bf16),
            dma((3,)), dma((C,)),
        ),
        out_specs=hbm,
        name="last",
    )
    return result[None]


def solution(mesh):
    in_specs = (
        P(None, None, "gx", "gy"),
        P(None, None, None, None, both),
        P(),
        P(),
        P(),
        P(),
    )
    out_specs = P(None, None, "gx", "gy")
    return jax.shard_map(
        on_device, mesh=mesh, in_specs=in_specs, out_specs=out_specs, check_vma=False
    )
```

```python
import functools
import math

import jax
import jax.numpy as jnp
import ml_dtypes
import numpy as np
from jax import lax
from jax.experimental import pallas as pl
from jax.experimental.pallas import tpu as pltpu
from jax.sharding import PartitionSpec as P

NX = 2048
NY = 2048
C = 20
LAYERS = 2
ROWS = 128
COLS = 256
GROUPS = 5
WIDE = 384
BLOCK = 8 * C

f32 = jnp.float32
bf16 = jnp.bfloat16
both = ("gx", "gy")
SUMS = (jnp.float32, jnp.bfloat16)
MIXED = (jnp.bfloat16, jnp.bfloat16)


def wave(numbers, positions, length):
    product = numbers.astype(np.int64)[:, None] * positions.astype(np.int64)[None, :]
    scale = np.float32(2.0 * math.pi / length)
    angle = (product % length).astype(np.float32) * scale
    angle = angle.astype(np.float64)
    return np.cos(angle).astype(np.float32), np.sin(angle).astype(np.float32)


def halves(value):
    high = value.astype(ml_dtypes.bfloat16)
    low = (value - high.astype(np.float32)).astype(ml_dtypes.bfloat16)
    return high, low


ky_all = np.arange(32)
kx_all = np.concatenate([np.arange(32), np.arange(32) + NX - 32])


def forward_cols():
    cosine, sine = wave(ky_all, np.arange(NY), NY)
    cosine, sine = cosine.T.reshape(NY, 2, 1, 16), sine.T.reshape(NY, 2, 1, 16)
    first = np.stack([cosine, -sine], axis=3)
    second = np.stack([-sine, -cosine], axis=3)
    tables = [np.broadcast_to(t, (NY, 2, 4, 2, 16)).reshape(NY, 256) for t in (first, second)]
    return np.stack(tables).astype(ml_dtypes.bfloat16)


def forward_rows(before, count):
    out = np.zeros((16, 2, 64, 2 * count), ml_dtypes.bfloat16)
    for device in range(16):
        cosine, sine = wave(kx_all, np.arange(ROWS) + device * ROWS, NX)
        table = np.zeros((2, 64, count), np.float32)
        table[0, :, before : before + ROWS] = cosine
        table[1, :, before : before + ROWS] = sine
        high, low = halves(np.transpose(table, (1, 0, 2)).reshape(64, 2 * count))
        out[device, 0], out[device, 1] = high, low
    return out


def inverse_rows(before, count):
    out = np.zeros((16, 2, count, 128), ml_dtypes.bfloat16)
    for device in range(16):
        positions = (np.arange(count) - before + device * ROWS) % NX
        cosine, sine = wave(kx_all, positions, NX)
        high, low = halves(np.concatenate([cosine.T, -sine.T], axis=1))
        out[device, 0], out[device, 1] = high, low
    return out


def inverse_cols():
    width = COLS
    out = np.zeros((8, 2, 64, 2 * width), ml_dtypes.bfloat16)
    weight = (np.where(ky_all == 0, 1.0, 2.0) / (NX * NY)).astype(np.float32)[:, None]
    for device in range(8):
        cosine, sine = wave(ky_all, np.arange(width) + device * COLS, NY)
        cosine, sine = cosine * weight, sine * weight
        real = np.concatenate([cosine, sine], axis=1)
        imaginary = np.concatenate([-sine, cosine], axis=1)
        table = np.stack([real.reshape(2, 16, 2 * width), imaginary.reshape(2, 16, 2 * width)], 1)
        high, low = halves(table.reshape(64, 2 * width))
        out[device, 0], out[device, 1] = high, low
    return out


def spread(taps):
    width = 2 * taps * BLOCK
    lanes = np.arange(width) % (taps * BLOCK) // 8
    return (np.arange(taps * C)[:, None] == lanes[None, :]).astype(ml_dtypes.bfloat16)


def offsets(taps):
    width = 2 * taps * BLOCK
    lanes = np.arange(width)
    place = lanes // (taps * BLOCK) * 8 + lanes % 8
    return (place[None, :] - np.arange(8)[:, None] - 4).astype(np.int32)


def split(value):
    high = value.astype(bf16)
    return high, (value - high.astype(f32)).astype(bf16)


def mul(a, b):
    return jnp.dot(a, b, preferred_element_type=f32)


def fetch(pairs):
    copies = [pltpu.make_async_copy(source, target, sem) for source, target, sem in pairs]
    for copy in copies:
        copy.start()
    return copies


def transform(planes, cols_ref, rows_ref, write):
    lane = lax.broadcasted_iota(jnp.int32, (COLS, 256), 1)
    slot = (lane >> 5) & 3
    zero = jnp.zeros((), bf16)
    rows_high, rows_low = rows_ref[0], rows_ref[1]
    members = jnp.concatenate(
        [
            jnp.concatenate([planes(4 * group + i) for group in range(GROUPS)], axis=0)
            for i in range(4)
        ],
        axis=1,
    )
    sums = []
    for t in range(2):
        placed = [jnp.where(slot == i, cols_ref[t], zero) for i in range(4)]
        sums.append(mul(members, jnp.concatenate(placed, axis=0)))
    count = members.shape[0] // GROUPS
    for group in range(GROUPS):
        own = [total[group * count : group * count + count] for total in sums]
        high, low = split(jnp.concatenate(own, axis=0))
        modes = mul(rows_high, high) + mul(rows_high, low) + mul(rows_low, high)
        for half in range(2):
            write(half, group, modes[:, 128 * half : 128 * half + 128])


def indices():
    return lax.axis_index("gx"), lax.axis_index("gy")


def forward_kernel(
    grid_all, cols_all, rows_all, out_ref, upper_ref, lower_ref, grid_buffer, chunk, cols, rows,
    sems,
):
    gx, gy = indices()
    start = pl.multiple_of(gy * COLS, COLS)
    copies = fetch(
        [
            (cols_all.at[:, pl.ds(start, COLS), :], cols, sems.at[0]),
            (rows_all.at[0, gx, :, :, pl.ds(0, 2 * ROWS)], rows, sems.at[1]),
        ]
        + [
            (grid_all.at[pl.ds(4 * g, 4)], grid_buffer.at[pl.ds(4 * g, 4)], sems.at[2 + g])
            for g in range(GROUPS)
        ]
        + [
            (grid_all.at[:, pl.ds(0, 8)], upper_ref, sems.at[2 + GROUPS]),
            (grid_all.at[:, pl.ds(ROWS - 8, 8)], lower_ref, sems.at[3 + GROUPS]),
        ]
    )
    for copy in copies:
        copy.wait()

    def write(half, group, value):
        chunk[pl.ds(half, 64, stride=2), group, :] = value

    transform(lambda c: grid_buffer[c], cols, rows, write)
    out_ref[...] = chunk[...].astype(out_ref.dtype)


def mixture_of(logits_ref, layer):
    exponents = jnp.exp(logits_ref[layer : layer + 1, :])
    weights = exponents / jnp.sum(exponents, axis=1, keepdims=True)
    return [weights[:, i : i + 1] for i in range(3)]


def mix_kernel(logits_ref, received_ref, weights_all, order_ref, out_ref, marker_ref, weights_ref, sem, *, layer):
    (copy,) = fetch([(weights_all.at[layer], weights_ref, sem)])
    total = jnp.sum(received_ref[...].astype(f32), axis=0)
    total = jnp.concatenate([total, jnp.zeros((8 - GROUPS, 128), f32)], axis=0)
    columns = jnp.transpose(total)
    real = jnp.zeros((16, C), f32)
    imaginary = jnp.zeros((16, C), f32)
    copy.wait()
    for c in range(C):
        group, start = c // 4, c % 4 * 32
        in_real = columns[start : start + 16, group : group + 1]
        in_imaginary = columns[start + 16 : start + 32, group : group + 1]
        weight_real, weight_imaginary = weights_ref[0, c], weights_ref[1, c]
        real = real + weight_real * in_real - weight_imaginary * in_imaginary
        imaginary = imaginary + weight_real * in_imaginary + weight_imaginary * in_real
    scale = mixture_of(logits_ref, layer)[0]
    lines = jnp.transpose(jnp.concatenate([real * scale, imaginary * scale] * 4, axis=0))
    lane = lax.broadcasted_iota(jnp.int32, (C, 128), 1)
    row = lax.broadcasted_iota(jnp.int32, (C, 128), 0)
    lines = jnp.where((lane >> 5) == (row & 3), lines, 0.0)
    group = lax.broadcasted_iota(jnp.int32, (8, C), 0)
    member = lax.broadcasted_iota(jnp.int32, (8, C), 1)
    gather = jnp.where((member >> 2) == group, 1.0, 0.0)
    mixed = jnp.dot(gather, lines, precision=lax.Precision.HIGHEST, preferred_element_type=f32)
    mixed = mixed[:GROUPS].astype(out_ref.dtype)
    out_ref[...] = jnp.broadcast_to(mixed[None], out_ref.shape)
    marker_ref[...] = lines[:8]


def edge_patterns():
    pick = lax.broadcasted_iota(jnp.int32, (8, COLS), 1) - lax.broadcasted_iota(
        jnp.int32, (8, COLS), 0
    )
    first = jnp.where(pick == 0, 1.0, 0.0).astype(bf16)
    last = jnp.where(pick == COLS - 8, 1.0, 0.0).astype(bf16)
    return first, last


def edge_columns(rows):
    dims = (((1,), (1,)), ((), ()))
    return [
        lax.dot_general(pattern, rows, dims, preferred_element_type=f32).astype(bf16)
        for pattern in edge_patterns()
    ]


def edges(rows, first_ref, last_ref):
    first_ref[...], last_ref[...] = edge_columns(rows)


def banded(weights, spread_ref, offsets_ref, steps, width):
    offset = offsets_ref[...][None]
    total = jnp.zeros((C, 8, width), f32)
    taps = len(steps) * C
    for index, step in enumerate(steps):
        own = mul(weights[:, taps * index : taps * index + taps], spread_ref[...])
        total = jnp.where(offset == step, own[:, None, :], total)
    return total.reshape(BLOCK, width).astype(bf16)


NEAR = (-1, 0, 1)
FAR = (-4, -2, 0, 2, 4)
ENDS_LAST = (7, 15, 19)
ENDS = {17: (8, 14, 17), 8: (5, 8)}


def own_kernel(
    grid_all, near_ref, far_ref, near_spread, far_spread, near_offsets, far_offsets, order_ref,
    field_all, first_ref, last_ref, near_band, far_band, grid_ref, field, sems, out_sem,
):
    pieces = [pl.ds(4 * g, 4) for g in range(GROUPS)]
    copies = fetch([(grid_all.at[p], grid_ref.at[p], sems.at[g]) for g, p in enumerate(pieces)])
    near_band[...] = banded(near_ref[0], near_spread, near_offsets, NEAR, 6 * BLOCK)
    far_band[...] = banded(far_ref[0], far_spread, far_offsets, FAR, 10 * BLOCK)
    for copy in copies:
        copy.wait()
    for pair in range(C // 2):
        inner = [grid_ref[2 * pair + i].astype(f32) for i in range(2)]
        for block in range(16):
            value = [v[8 * block : 8 * block + 8] for v in inner]
            place = block * BLOCK + 16 * pair
            field[place : place + 16, :] = jnp.concatenate(value, axis=0).astype(bf16)
    (result,) = fetch([(field, field_all, out_sem)])
    edges(field[...], first_ref, last_ref)
    result.wait()


def edges_kernel(top_ref, bottom_ref, first_ref, last_ref, first_out, last_out):
    found = edge_columns(jnp.concatenate([top_ref[...], bottom_ref[...]], axis=0))
    for own_ref, extra, out_ref in zip((first_ref, last_ref), found, (first_out, last_out)):
        out_ref[:, : C * ROWS] = own_ref[...]
        out_ref[:, C * ROWS :] = extra


def conv_kernel(logits_ref, *refs, layer, first, count):
    if layer == 0:
        main_all, top_all, bottom_all, left_ref, right_ref, near_all, far_all, *refs = refs
        order_ref, out_all, marker_ref, *refs = refs
    else:
        field_all, left_ref, right_ref, near_ref, far_ref, near_spread, far_spread, *refs = refs
        near_offsets, far_offsets, order_ref, out_all, marker_ref, *refs = refs
    field, out_ref, near_band, far_band, near_stack, far_stack, sems, out_sems = refs
    if layer == 0:
        copies = fetch(
            [
                (top_all, field.at[pl.ds(0, BLOCK)], sems.at[0]),
                (main_all, field.at[pl.ds(BLOCK, 16 * BLOCK)], sems.at[1]),
                (bottom_all, field.at[pl.ds(17 * BLOCK, BLOCK)], sems.at[2]),
                (near_all, near_band, sems.at[3]),
                (far_all, far_band, sems.at[4]),
            ]
        )
    else:
        piece = pl.ds(first * BLOCK, (count + 1) * BLOCK)
        copies = fetch([(field_all.at[piece], field, sems.at[0])])
        near_band[...] = banded(near_ref[layer], near_spread, near_offsets, NEAR, 6 * BLOCK)
        far_band[...] = banded(far_ref[layer], far_spread, far_offsets, FAR, 10 * BLOCK)
    lane = lax.broadcasted_iota(jnp.int32, (16, 128), 1)
    row = lax.broadcasted_iota(jnp.int32, (16, 128), 0)
    sides_place = jnp.where(lane == jnp.where(row < 8, row, row + 112), 1.0, 0.0).astype(bf16)
    lanes = slice(first * BLOCK, (first + count + 1) * BLOCK)
    sides = [r[:, lanes].astype(f32) for r in (right_ref, left_ref)]
    sides = jnp.concatenate(sides, axis=0)
    side = lax.dot_general(
        sides.astype(bf16), sides_place, (((0,), (0,)), ((), ())), preferred_element_type=f32
    )
    side = side.astype(bf16)
    for copy in copies:
        copy.wait()

    def side_of(block):
        start = block * BLOCK
        if layer == 0:
            start = {0: 16 * BLOCK, 17: 17 * BLOCK}.get(block, start - BLOCK)
        return side[start : start + BLOCK]

    _, near_scale, far_scale = mixture_of(logits_ref, layer)
    results = []
    for index in range(count + 1):
        rows = slice(index * BLOCK, index * BLOCK + BLOCK)
        block = jnp.concatenate([field[rows, :], side_of(index)], axis=1)
        moved = {0: block}
        for step in (-4, -2, -1, 1, 2, 4):
            moved[step] = pltpu.roll(block, (-step) % WIDE, 1)
        for steps, stack in ((NEAR, near_stack), (FAR, far_stack)):
            for position, step in enumerate(steps):
                start = (index * len(steps) + position) * BLOCK
                stack[start : start + BLOCK, :] = moved[step][:, :COLS]
        if index == 0:
            continue
        done = index - 1
        near_rows = near_stack[done * 3 * BLOCK : (done + 2) * 3 * BLOCK, :]
        far_rows = far_stack[done * 5 * BLOCK : (done + 2) * 5 * BLOCK, :]
        total = near_scale * mul(near_band[...], near_rows) + far_scale * mul(
            far_band[...], far_rows
        )
        out_ref[:, 8 * done : 8 * done + 8, :] = total.reshape(C, 8, COLS)
        if done + 1 in ENDS[count]:
            start = max((e for e in ENDS[count] if e < done + 1), default=0)
            piece = pl.ds(8 * start, 8 * (done + 1 - start))
            results += fetch(
                [(out_ref.at[:, piece], out_all.at[:, piece], out_sems.at[len(results)])]
            )
    marker_ref[...] = total[:8, :128]
    for copy in results:
        copy.wait()


def gelu(value):
    return 0.5 * value * (1.0 + lax.erf(value * math.sqrt(0.5)))


def expand(bias_ref, gathered, cols, rows, lines, conv_ref, arrive, layer, emit):
    parts = []
    for group in range(GROUPS):
        pair = [gathered[pl.ds(half, 64, stride=2), group, :] for half in range(2)]
        parts.append(jnp.concatenate(pair, axis=1))
    high, low = split(jnp.concatenate(parts, axis=0))
    stacked = jnp.concatenate([high, low], axis=0)
    rows_high, rows_low = rows[0], rows[1]
    rows_twice = jnp.concatenate([rows_high, rows_high], axis=1)
    empty = jnp.zeros((32, 2 * COLS), bf16)
    for slot in range(4):
        placed = []
        for t in range(2):
            table = cols[t]
            pieces = []
            for half in range(2):
                own = table[32 * half : 32 * half + 32]
                pieces += [own if i == slot else empty for i in range(4)]
            placed.append(jnp.concatenate(pieces, axis=0))
        first = mul(stacked, placed[0])
        lines[slot] = first[:320] + first[320:] + mul(high, placed[1])
    arrive()
    for channel in range(C):
        group, slot = channel // 4, channel % 4
        here = lines[slot, 64 * group : 64 * group + 64]
        line_high, line_low = split(jnp.concatenate([here[:, :COLS], here[:, COLS:]], axis=0))
        value = mul(rows_twice, jnp.concatenate([line_high, line_low], axis=0)) + mul(
            rows_low, line_high
        )
        emit(channel, gelu(value + conv_ref[channel] + bias_ref[layer, channel]))


def middle_kernel(
    bias_ref, gathered_ref, icols_all, irows_all, fcols_all, frows_all, conv_all,
    field_all, first_ref, last_ref, out_ref,
    planes, chunk, icols, irows, fcols, frows, conv_ref, field_ref, lines, sems, conv_sem,
    field_sems,
):
    gx, gy = indices()
    start = pl.multiple_of(gy * COLS, COLS)
    copies = fetch(
        [
            (icols_all.at[0, gy], icols, sems.at[0]),
            (irows_all.at[1, gx], irows, sems.at[1]),
            (fcols_all.at[:, pl.ds(start, COLS), :], fcols, sems.at[2]),
            (frows_all.at[1, gx], frows, sems.at[3]),
        ]
    )
    (arrival,) = fetch([(conv_all, conv_ref, conv_sem)])
    chunk[...] = gathered_ref[...].astype(f32)
    copies[0].wait()
    copies[1].wait()
    waiting = []
    results = []

    def emit(channel, value):
        rounded = value.astype(bf16)
        planes[channel, :136] = rounded
        planes[channel, 136:] = jnp.zeros((8, COLS), bf16)
        waiting.append(rounded.astype(f32))
        if channel % 2 == 1:
            for block in range(17):
                rows = slice(8 * block, 8 * block + 8)
                both_rows = jnp.concatenate([waiting[0][rows], waiting[1][rows]], axis=0)
                place = 8 * (channel - 1)
                field_ref[block, place : place + 16, :] = both_rows.astype(bf16)
            waiting.clear()
        if channel in (9, 19):
            piece = pl.ds(8 * (channel - 9), 80)
            sem = field_sems.at[len(results)]
            results.extend(fetch([(field_ref.at[:, piece], field_all.at[:, piece], sem)]))

    expand(bias_ref, chunk, icols, irows, lines, conv_ref, arrival.wait, 0, emit)
    edges(field_ref[...].reshape(17 * BLOCK, COLS), first_ref, last_ref)
    copies[2].wait()
    copies[3].wait()

    def write(half, group, value):
        chunk[pl.ds(half, 64, stride=2), group, :] = value

    transform(lambda c: planes[c], fcols, frows, write)
    out_ref[...] = chunk[...].astype(out_ref.dtype)
    for copy in results:
        copy.wait()


def last_kernel(
    bias_ref, gathered_ref, icols_all, irows_all, upper_all, lower_all, out_all,
    wide, icols, irows, conv_ref, out_ref, lines, sems, conv_sems, out_sems,
):
    gx, gy = indices()
    copies = fetch(
        [
            (icols_all.at[0, gy], icols, sems.at[0]),
            (irows_all.at[0, gx, :, pl.ds(0, ROWS)], irows, sems.at[1]),
        ]
    )
    arrivals = fetch(
        [
            (upper_all, conv_ref.at[:, pl.ds(0, 64)], conv_sems.at[0]),
            (lower_all, conv_ref.at[:, pl.ds(64, 64)], conv_sems.at[1]),
        ]
    )
    wide[...] = gathered_ref[...].astype(f32)
    copies[0].wait()
    copies[1].wait()
    results = []

    def emit(channel, value):
        out_ref[channel] = value.astype(bf16)
        if channel in ENDS_LAST:
            start = max((e + 1 for e in ENDS_LAST if e < channel), default=0)
            piece = pl.ds(start, channel + 1 - start)
            sem = out_sems.at[len(results)]
            results.extend(fetch([(out_ref.at[piece], out_all.at[piece], sem)]))

    def arrive():
        for copy in arrivals:
            copy.wait()

    expand(bias_ref, wide, icols, irows, lines, conv_ref, arrive, 1, emit)
    for copy in results:
        copy.wait()


vmem = pl.BlockSpec(memory_space=pltpu.VMEM)
smem = pl.BlockSpec(memory_space=pltpu.SMEM)
anywhere = pl.BlockSpec(memory_space=pl.ANY)
hbm = pl.BlockSpec(memory_space=pltpu.HBM)
LIMIT = 56 * 10**6
SMALL = 4 * 10**6


def call(kernel, outs, args, specs, scratch=(), out_specs=None, flops=10**9, limit=LIMIT, name=None):
    single = not isinstance(outs, (list, tuple))
    if out_specs is None:
        out_specs = vmem if single else [vmem] * len(outs)
    return pl.pallas_call(
        kernel,
        out_shape=outs,
        in_specs=specs,
        out_specs=out_specs,
        scratch_shapes=list(scratch),
        compiler_params=pltpu.CompilerParams(vmem_limit_bytes=limit),
        cost_estimate=pl.CostEstimate(flops=flops, bytes_accessed=4 * 10**6, transcendentals=0),
        name=name,
    )(*args)


def shape_of(dims, kind):
    return jax.ShapeDtypeStruct(dims, kind)


def exchange(value):
    return lax.all_to_all(value, both, split_axis=0, concat_axis=0, tiled=True)


def ring(axis, step):
    size = lax.axis_size(axis)
    return [(i, (i + step) % size) for i in range(size)]


def sides(first, last):
    left = lax.ppermute(last, "gy", ring("gy", 1))
    right = lax.ppermute(first, "gy", ring("gy", -1))
    return left, right


def on_device(grid_field, spectral_weight, conv_near, conv_far, mix_logits, channel_bias):
    grid = grid_field[0]
    mode_weights = jnp.swapaxes(spectral_weight, 3, 4)

    fcols = jnp.asarray(forward_cols())
    plain, wide = forward_rows(0, ROWS), forward_rows(4, 144)
    frows = np.zeros((2,) + wide.shape, wide.dtype)
    frows[0, ..., : 2 * ROWS], frows[1] = plain, wide
    plain, wide = inverse_rows(0, ROWS), inverse_rows(4, 136)
    irows = np.zeros((2,) + wide.shape, wide.dtype)
    irows[0, :, :, :ROWS], irows[1] = plain, wide
    icols = np.stack([inverse_cols()] * 2)
    frows, irows, icols = jnp.asarray(frows), jnp.asarray(irows), jnp.asarray(icols)

    chunks = [shape_of((128, GROUPS, 128), kind) for kind in SUMS]
    answers = [shape_of((128, GROUPS, 128), kind) for kind in MIXED]
    dma = pltpu.SemaphoreType.DMA
    icols_buffer = pltpu.VMEM((2, 64, 2 * COLS), bf16)
    fcols_buffer = pltpu.VMEM((2, COLS, 256), bf16)

    partial, upper, lower = call(
        forward_kernel, [chunks[0]] + [shape_of((C, 8, COLS), bf16)] * 2, (grid, fcols, frows),
        [hbm] * 3,
        (
            pltpu.VMEM((C, ROWS, COLS), bf16), pltpu.VMEM((128, GROUPS, 128), f32), fcols_buffer,
            pltpu.VMEM((2, 64, 2 * ROWS), bf16),
            dma((4 + GROUPS,)),
        ),
        name="forward",
    )
    top = lax.ppermute(lower, "gx", ring("gx", 1)).reshape(BLOCK, COLS)
    bottom = lax.ppermute(upper, "gx", ring("gx", -1)).reshape(BLOCK, COLS)
    received = exchange(partial)
    tables = [jnp.asarray(t) for t in (spread(3), spread(5), offsets(3), offsets(5))]
    near_shape, far_shape = (BLOCK, 6 * BLOCK), (BLOCK, 10 * BLOCK)
    field, first, last, near_band, far_band = call(
        own_kernel,
        [shape_of((16 * BLOCK, COLS), bf16)] + [shape_of((8, 16 * BLOCK), bf16)] * 2
        + [shape_of(near_shape, bf16), shape_of(far_shape, bf16)],
        (grid, conv_near, conv_far, *tables, upper), [hbm] + [vmem] * 6 + [anywhere],
        (
            pltpu.VMEM((C, ROWS, COLS), bf16), pltpu.VMEM((16 * BLOCK, COLS), bf16),
            dma((GROUPS,)), dma,
        ),
        out_specs=[hbm] + [vmem] * 4, name="own",
    )
    first, last = call(
        edges_kernel, [shape_of((8, 18 * BLOCK), bf16)] * 2, (top, bottom, first, last),
        [vmem] * 4, limit=SMALL, name="edges",
    )

    def mix(layer, received, order):
        return call(
            functools.partial(mix_kernel, layer=layer), [answers[layer], shape_of((8, 128), f32)],
            (mix_logits, received, mode_weights, order), [vmem, vmem, hbm, anywhere],
            (pltpu.VMEM((2, C, 16, C), f32), dma), flops=10**6, limit=SMALL, name="mix",
        )

    def conv(layer, sources, specs, first, count, order):
        return call(
            functools.partial(conv_kernel, layer=layer, first=first, count=count),
            [shape_of((C, 8 * count, COLS), f32), shape_of((8, 128), f32)],
            (mix_logits, *sources, order), [vmem] + specs + [anywhere],
            (
                pltpu.VMEM(((count + 1) * BLOCK, COLS), bf16),
                pltpu.VMEM((C, 8 * count, COLS), f32),
                pltpu.VMEM(near_shape, bf16),
                pltpu.VMEM(far_shape, bf16),
                pltpu.VMEM(((count + 1) * 3 * BLOCK, COLS), bf16),
                pltpu.VMEM(((count + 1) * 5 * BLOCK, COLS), bf16),
                dma((5,)), dma((3,)),
            ),
            out_specs=[hbm, vmem], flops=2 * 10**10, name="conv",
        )

    around = sides(first, last)
    mixed, marker = mix(0, received, mix_logits)
    gathered = exchange(mixed)
    specs = [hbm] * 3 + [vmem] * 2 + [hbm] * 2
    local, _ = conv(0, (field, top, bottom, *around, near_band, far_band), specs, 0, 17, marker)
    field, first, last, partial = call(
        middle_kernel,
        [shape_of((17, BLOCK, COLS), bf16)] + [shape_of((8, 17 * BLOCK), bf16)] * 2 + [chunks[1]],
        (channel_bias, gathered, icols, irows, fcols, frows, local),
        [smem, vmem] + [hbm] * 5,
        (
            pltpu.VMEM((C, 144, COLS), bf16), pltpu.VMEM((128, GROUPS, 128), f32),
            icols_buffer, pltpu.VMEM((2, 136, 128), bf16),
            fcols_buffer, pltpu.VMEM((2, 64, 288), bf16),
            pltpu.VMEM((C, 136, COLS), f32), pltpu.VMEM((17, BLOCK, COLS), bf16),
            pltpu.VMEM((4, 320, 2 * COLS), f32), dma((4,)), dma, dma((2,)),
        ),
        out_specs=[hbm, vmem, vmem, vmem],
        name="middle",
    )
    received = exchange(partial)
    field, around = field.reshape(17 * BLOCK, COLS), sides(first, last)
    sources, specs = (field, *around, conv_near, conv_far, *tables), [hbm] + [vmem] * 8
    upper, marker = conv(1, sources, specs, 0, 8, mix_logits)
    mixed, marker = mix(1, received, marker)
    gathered = exchange(mixed)
    lower, _ = conv(1, sources, specs, 8, 8, marker)
    result = call(
        last_kernel, shape_of((C, ROWS, COLS), bf16),
        (channel_bias, gathered, icols, irows, upper, lower),
        [smem, vmem] + [hbm] * 4,
        (
            pltpu.VMEM((128, GROUPS, 128), f32), icols_buffer, pltpu.VMEM((2, ROWS, 128), bf16),
            pltpu.VMEM((C, ROWS, COLS), f32), pltpu.VMEM((C, ROWS, COLS), bf16),
            pltpu.VMEM((4, 320, 2 * COLS), f32), dma((2,)), dma((2,)), dma((3,)),
        ),
        out_specs=hbm,
        name="last",
    )
    return result[None]


def solution(mesh):
    in_specs = (
        P(None, None, "gx", "gy"),
        P(None, None, None, None, both),
        P(),
        P(),
        P(),
        P(),
    )
    out_specs = P(None, None, "gx", "gy")
    return jax.shard_map(
        on_device, mesh=mesh, in_specs=in_specs, out_specs=out_specs, check_vma=False
    )
```

```python
import functools
import math

import jax
import jax.numpy as jnp
import ml_dtypes
import numpy as np
from jax import lax
from jax.experimental import pallas as pl
from jax.experimental.pallas import tpu as pltpu
from jax.sharding import PartitionSpec as P

NX = 2048
NY = 2048
C = 20
LAYERS = 2
ROWS = 128
COLS = 256
GROUPS = 5
WIDE = 384
BLOCK = 8 * C

f32 = jnp.float32
bf16 = jnp.bfloat16
both = ("gx", "gy")
SUMS = (jnp.float32, jnp.bfloat16)
MIXED = (jnp.bfloat16, jnp.bfloat16)


def wave(numbers, positions, length):
    product = numbers.astype(np.int64)[:, None] * positions.astype(np.int64)[None, :]
    scale = np.float32(2.0 * math.pi / length)
    angle = (product % length).astype(np.float32) * scale
    angle = angle.astype(np.float64)
    return np.cos(angle).astype(np.float32), np.sin(angle).astype(np.float32)


def halves(value):
    high = value.astype(ml_dtypes.bfloat16)
    low = (value - high.astype(np.float32)).astype(ml_dtypes.bfloat16)
    return high, low


ky_all = np.arange(32)
kx_all = np.concatenate([np.arange(32), np.arange(32) + NX - 32])


def forward_cols():
    cosine, sine = wave(ky_all, np.arange(NY), NY)
    cosine, sine = cosine.T.reshape(NY, 2, 1, 16), sine.T.reshape(NY, 2, 1, 16)
    first = np.stack([cosine, -sine], axis=3)
    second = np.stack([-sine, -cosine], axis=3)
    tables = [np.broadcast_to(t, (NY, 2, 4, 2, 16)).reshape(NY, 256) for t in (first, second)]
    return np.stack(tables).astype(ml_dtypes.bfloat16)


def forward_rows(before, count):
    out = np.zeros((16, 2, 64, 2 * count), ml_dtypes.bfloat16)
    for device in range(16):
        cosine, sine = wave(kx_all, np.arange(ROWS) + device * ROWS, NX)
        table = np.zeros((2, 64, count), np.float32)
        table[0, :, before : before + ROWS] = cosine
        table[1, :, before : before + ROWS] = sine
        high, low = halves(np.transpose(table, (1, 0, 2)).reshape(64, 2 * count))
        out[device, 0], out[device, 1] = high, low
    return out


def inverse_rows(before, count):
    out = np.zeros((16, 2, count, 128), ml_dtypes.bfloat16)
    for device in range(16):
        positions = (np.arange(count) - before + device * ROWS) % NX
        cosine, sine = wave(kx_all, positions, NX)
        high, low = halves(np.concatenate([cosine.T, -sine.T], axis=1))
        out[device, 0], out[device, 1] = high, low
    return out


def inverse_cols():
    width = COLS
    out = np.zeros((8, 2, 64, 2 * width), ml_dtypes.bfloat16)
    weight = (np.where(ky_all == 0, 1.0, 2.0) / (NX * NY)).astype(np.float32)[:, None]
    for device in range(8):
        cosine, sine = wave(ky_all, np.arange(width) + device * COLS, NY)
        cosine, sine = cosine * weight, sine * weight
        real = np.concatenate([cosine, sine], axis=1)
        imaginary = np.concatenate([-sine, cosine], axis=1)
        table = np.stack([real.reshape(2, 16, 2 * width), imaginary.reshape(2, 16, 2 * width)], 1)
        high, low = halves(table.reshape(64, 2 * width))
        out[device, 0], out[device, 1] = high, low
    return out


def spread(taps):
    width = 2 * taps * BLOCK
    lanes = np.arange(width) % (taps * BLOCK) // 8
    return (np.arange(taps * C)[:, None] == lanes[None, :]).astype(ml_dtypes.bfloat16)


def offsets(taps):
    width = 2 * taps * BLOCK
    lanes = np.arange(width)
    place = lanes // (taps * BLOCK) * 8 + lanes % 8
    return (place[None, :] - np.arange(8)[:, None] - 4).astype(np.int32)


def split(value):
    high = value.astype(bf16)
    return high, (value - high.astype(f32)).astype(bf16)


def mul(a, b):
    return jnp.dot(a, b, preferred_element_type=f32)


def fetch(pairs):
    copies = [pltpu.make_async_copy(source, target, sem) for source, target, sem in pairs]
    for copy in copies:
        copy.start()
    return copies


def transform(planes, cols_ref, rows_ref, write):
    lane = lax.broadcasted_iota(jnp.int32, (COLS, 256), 1)
    slot = (lane >> 5) & 3
    zero = jnp.zeros((), bf16)
    rows_high, rows_low = rows_ref[0], rows_ref[1]
    members = jnp.concatenate(
        [
            jnp.concatenate([planes(4 * group + i) for group in range(GROUPS)], axis=0)
            for i in range(4)
        ],
        axis=1,
    )
    sums = []
    for t in range(2):
        placed = [jnp.where(slot == i, cols_ref[t], zero) for i in range(4)]
        sums.append(mul(members, jnp.concatenate(placed, axis=0)))
    count = members.shape[0] // GROUPS
    for group in range(GROUPS):
        own = [total[group * count : group * count + count] for total in sums]
        high, low = split(jnp.concatenate(own, axis=0))
        modes = mul(rows_high, high) + mul(rows_high, low) + mul(rows_low, high)
        for half in range(2):
            write(half, group, modes[:, 128 * half : 128 * half + 128])


def indices():
    return lax.axis_index("gx"), lax.axis_index("gy")


def forward_kernel(
    grid_all, cols_all, rows_all, out_ref, upper_ref, lower_ref, grid_buffer, cols, rows, sems
):
    gx, gy = indices()
    start = pl.multiple_of(gy * COLS, COLS)
    copies = fetch(
        [
            (cols_all.at[:, pl.ds(start, COLS), :], cols, sems.at[0]),
            (rows_all.at[0, gx, :, :, pl.ds(0, 2 * ROWS)], rows, sems.at[1]),
        ]
        + [
            (grid_all.at[pl.ds(4 * g, 4)], grid_buffer.at[pl.ds(4 * g, 4)], sems.at[2 + g])
            for g in range(GROUPS)
        ]
        + [
            (grid_all.at[:, pl.ds(0, 8)], upper_ref, sems.at[2 + GROUPS]),
            (grid_all.at[:, pl.ds(ROWS - 8, 8)], lower_ref, sems.at[3 + GROUPS]),
        ]
    )
    for copy in copies:
        copy.wait()

    def write(half, group, value):
        out_ref[pl.ds(half, 64, stride=2), group, :] = value

    transform(lambda c: grid_buffer[c], cols, rows, write)


def mixture_of(logits_ref, layer):
    exponents = jnp.exp(logits_ref[layer : layer + 1, :])
    weights = exponents / jnp.sum(exponents, axis=1, keepdims=True)
    return [weights[:, i : i + 1] for i in range(3)]


def mix_kernel(logits_ref, received_ref, weights_all, order_ref, out_ref, marker_ref, weights_ref, sem, *, layer):
    (copy,) = fetch([(weights_all.at[layer], weights_ref, sem)])
    total = jnp.sum(received_ref[...].astype(f32), axis=0)
    total = jnp.concatenate([total, jnp.zeros((8 - GROUPS, 128), f32)], axis=0)
    columns = jnp.transpose(total)
    real = jnp.zeros((16, C), f32)
    imaginary = jnp.zeros((16, C), f32)
    copy.wait()
    for c in range(C):
        group, start = c // 4, c % 4 * 32
        in_real = columns[start : start + 16, group : group + 1]
        in_imaginary = columns[start + 16 : start + 32, group : group + 1]
        weight_real, weight_imaginary = weights_ref[0, c], weights_ref[1, c]
        real = real + weight_real * in_real - weight_imaginary * in_imaginary
        imaginary = imaginary + weight_real * in_imaginary + weight_imaginary * in_real
    scale = mixture_of(logits_ref, layer)[0]
    lines = jnp.transpose(jnp.concatenate([real * scale, imaginary * scale] * 4, axis=0))
    lane = lax.broadcasted_iota(jnp.int32, (C, 128), 1)
    row = lax.broadcasted_iota(jnp.int32, (C, 128), 0)
    lines = jnp.where((lane >> 5) == (row & 3), lines, 0.0)
    group = lax.broadcasted_iota(jnp.int32, (8, C), 0)
    member = lax.broadcasted_iota(jnp.int32, (8, C), 1)
    gather = jnp.where((member >> 2) == group, 1.0, 0.0)
    mixed = jnp.dot(gather, lines, precision=lax.Precision.HIGHEST, preferred_element_type=f32)
    mixed = mixed[:GROUPS].astype(out_ref.dtype)
    out_ref[...] = jnp.broadcast_to(mixed[None], out_ref.shape)
    marker_ref[...] = lines[:8]


def edge_patterns():
    pick = lax.broadcasted_iota(jnp.int32, (8, COLS), 1) - lax.broadcasted_iota(
        jnp.int32, (8, COLS), 0
    )
    first = jnp.where(pick == 0, 1.0, 0.0).astype(bf16)
    last = jnp.where(pick == COLS - 8, 1.0, 0.0).astype(bf16)
    return first, last


def edge_columns(rows):
    patterns = [p.astype(f32) for p in edge_patterns()]
    patterns = jnp.concatenate(patterns, axis=0).astype(bf16)
    found = lax.dot_general(
        patterns, rows, (((1,), (1,)), ((), ())), preferred_element_type=f32
    )
    return found[:8].astype(bf16), found[8:].astype(bf16)


def edges(rows, first_ref, last_ref):
    first_ref[...], last_ref[...] = edge_columns(rows)


def banded(weights, spread_ref, offsets_ref, steps, width):
    offset = offsets_ref[...][None]
    total = jnp.zeros((C, 8, width), f32)
    taps = len(steps) * C
    for index, step in enumerate(steps):
        own = mul(weights[:, taps * index : taps * index + taps], spread_ref[...])
        total = jnp.where(offset == step, own[:, None, :], total)
    return total.reshape(BLOCK, width).astype(bf16)


NEAR = (-1, 0, 1)
FAR = (-4, -2, 0, 2, 4)
ENDS_LAST = (4, 9, 14, 17, 19)
ENDS = {17: (8, 14, 17), 8: (5, 8)}


def own_kernel(
    grid_all, near_ref, far_ref, near_spread, far_spread, near_offsets, far_offsets, order_ref,
    field_all, first_ref, last_ref, near_band, far_band, grid_ref, field, sems, out_sem,
):
    pieces = [pl.ds(4 * g, 4) for g in range(GROUPS)]
    copies = fetch([(grid_all.at[p], grid_ref.at[p], sems.at[g]) for g, p in enumerate(pieces)])
    near_band[...] = banded(near_ref[0], near_spread, near_offsets, NEAR, 6 * BLOCK)
    far_band[...] = banded(far_ref[0], far_spread, far_offsets, FAR, 10 * BLOCK)
    for copy in copies:
        copy.wait()
    for pair in range(C // 2):
        inner = [grid_ref[2 * pair + i].astype(f32) for i in range(2)]
        for block in range(16):
            value = [v[8 * block : 8 * block + 8] for v in inner]
            place = block * BLOCK + 16 * pair
            field[place : place + 16, :] = jnp.concatenate(value, axis=0).astype(bf16)
    (result,) = fetch([(field, field_all, out_sem)])
    edges(field[...], first_ref, last_ref)
    result.wait()


def edges_kernel(top_ref, bottom_ref, first_ref, last_ref, first_out, last_out):
    found = edge_columns(jnp.concatenate([top_ref[...], bottom_ref[...]], axis=0))
    for own_ref, extra, out_ref in zip((first_ref, last_ref), found, (first_out, last_out)):
        out_ref[:, : C * ROWS] = own_ref[...]
        out_ref[:, C * ROWS :] = extra


def conv_kernel(logits_ref, *refs, layer, first, count):
    if layer == 0:
        main_all, top_all, bottom_all, left_ref, right_ref, near_all, far_all, *refs = refs
        order_ref, out_all, marker_ref, *refs = refs
    else:
        field_all, left_ref, right_ref, near_ref, far_ref, near_spread, far_spread, *refs = refs
        near_offsets, far_offsets, order_ref, out_all, marker_ref, *refs = refs
    field, out_ref, near_band, far_band, near_stack, far_stack, sems, out_sems = refs
    if layer == 0:
        copies = fetch(
            [
                (top_all, field.at[pl.ds(0, BLOCK)], sems.at[0]),
                (main_all, field.at[pl.ds(BLOCK, 16 * BLOCK)], sems.at[1]),
                (bottom_all, field.at[pl.ds(17 * BLOCK, BLOCK)], sems.at[2]),
                (near_all, near_band, sems.at[3]),
                (far_all, far_band, sems.at[4]),
            ]
        )
    else:
        piece = pl.ds(first * BLOCK, (count + 1) * BLOCK)
        copies = fetch([(field_all.at[piece], field, sems.at[0])])
        near_band[...] = banded(near_ref[layer], near_spread, near_offsets, NEAR, 6 * BLOCK)
        far_band[...] = banded(far_ref[layer], far_spread, far_offsets, FAR, 10 * BLOCK)
    lane = lax.broadcasted_iota(jnp.int32, (16, 128), 1)
    row = lax.broadcasted_iota(jnp.int32, (16, 128), 0)
    sides_place = jnp.where(lane == jnp.where(row < 8, row, row + 112), 1.0, 0.0).astype(bf16)
    lanes = slice(first * BLOCK, (first + count + 1) * BLOCK)
    sides = [r[:, lanes].astype(f32) for r in (right_ref, left_ref)]
    sides = jnp.concatenate(sides, axis=0)
    side = lax.dot_general(
        sides.astype(bf16), sides_place, (((0,), (0,)), ((), ())), preferred_element_type=f32
    )
    side = side.astype(bf16)
    for copy in copies:
        copy.wait()

    def side_of(block):
        start = block * BLOCK
        if layer == 0:
            start = {0: 16 * BLOCK, 17: 17 * BLOCK}.get(block, start - BLOCK)
        return side[start : start + BLOCK]

    _, near_scale, far_scale = mixture_of(logits_ref, layer)
    results = []
    for index in range(count + 1):
        rows = slice(index * BLOCK, index * BLOCK + BLOCK)
        block = jnp.concatenate([field[rows, :], side_of(index)], axis=1)
        moved = {0: block}
        for step in (-4, -2, -1, 1, 2, 4):
            moved[step] = pltpu.roll(block, (-step) % WIDE, 1)
        for steps, stack in ((NEAR, near_stack), (FAR, far_stack)):
            for position, step in enumerate(steps):
                start = (index * len(steps) + position) * BLOCK
                stack[start : start + BLOCK, :] = moved[step][:, :COLS]
        if index == 0:
            continue
        done = index - 1
        near_rows = near_stack[done * 3 * BLOCK : (done + 2) * 3 * BLOCK, :]
        far_rows = far_stack[done * 5 * BLOCK : (done + 2) * 5 * BLOCK, :]
        total = near_scale * mul(near_band[...], near_rows) + far_scale * mul(
            far_band[...], far_rows
        )
        out_ref[:, 8 * done : 8 * done + 8, :] = total.reshape(C, 8, COLS)
        if done + 1 in ENDS[count]:
            start = max((e for e in ENDS[count] if e < done + 1), default=0)
            piece = pl.ds(8 * start, 8 * (done + 1 - start))
            results += fetch(
                [(out_ref.at[:, piece], out_all.at[:, piece], out_sems.at[len(results)])]
            )
    marker_ref[...] = total[:8, :128]
    for copy in results:
        copy.wait()


def gelu(value):
    return 0.5 * value * (1.0 + lax.erf(value * math.sqrt(0.5)))


def expand(bias_ref, gathered, cols, rows, lines, conv_ref, arrive, layer, emit):
    parts = []
    for group in range(GROUPS):
        pair = [gathered[pl.ds(half, 64, stride=2), group, :] for half in range(2)]
        parts.append(jnp.concatenate(pair, axis=1))
    high, low = split(jnp.concatenate(parts, axis=0))
    stacked = jnp.concatenate([high, low], axis=0)
    rows_high, rows_low = rows[0], rows[1]
    rows_twice = jnp.concatenate([rows_high, rows_high], axis=1)
    empty = jnp.zeros((32, 2 * COLS), bf16)
    for slot in range(4):
        placed = []
        for t in range(2):
            table = cols[t]
            pieces = []
            for half in range(2):
                own = table[32 * half : 32 * half + 32]
                pieces += [own if i == slot else empty for i in range(4)]
            placed.append(jnp.concatenate(pieces, axis=0))
        first = mul(stacked, placed[0])
        lines[slot] = first[:320] + first[320:] + mul(high, placed[1])
    arrive()
    for channel in range(C):
        group, slot = channel // 4, channel % 4
        here = lines[slot, 64 * group : 64 * group + 64]
        line_high, line_low = split(jnp.concatenate([here[:, :COLS], here[:, COLS:]], axis=0))
        value = mul(rows_twice, jnp.concatenate([line_high, line_low], axis=0)) + mul(
            rows_low, line_high
        )
        emit(channel, gelu(value + conv_ref[channel] + bias_ref[layer, channel]))


def middle_kernel(
    bias_ref, gathered_ref, icols_all, irows_all, fcols_all, frows_all, conv_all,
    field_all, first_ref, last_ref, out_ref,
    planes, chunk, icols, irows, fcols, frows, conv_ref, field_ref, lines, sems, conv_sem,
    field_sems,
):
    gx, gy = indices()
    start = pl.multiple_of(gy * COLS, COLS)
    copies = fetch(
        [
            (icols_all.at[0, gy], icols, sems.at[0]),
            (irows_all.at[1, gx], irows, sems.at[1]),
            (fcols_all.at[:, pl.ds(start, COLS), :], fcols, sems.at[2]),
            (frows_all.at[1, gx], frows, sems.at[3]),
        ]
    )
    (arrival,) = fetch([(conv_all, conv_ref, conv_sem)])
    chunk[...] = gathered_ref[...].astype(f32)
    copies[0].wait()
    copies[1].wait()
    waiting = []
    results = []

    def emit(channel, value):
        rounded = value.astype(bf16)
        planes[channel, :136] = rounded
        planes[channel, 136:] = jnp.zeros((8, COLS), bf16)
        waiting.append(rounded.astype(f32))
        if channel % 2 == 1:
            for block in range(17):
                rows = slice(8 * block, 8 * block + 8)
                both_rows = jnp.concatenate([waiting[0][rows], waiting[1][rows]], axis=0)
                place = 8 * (channel - 1)
                field_ref[block, place : place + 16, :] = both_rows.astype(bf16)
            waiting.clear()
        if channel in (9, 19):
            piece = pl.ds(8 * (channel - 9), 80)
            sem = field_sems.at[len(results)]
            results.extend(fetch([(field_ref.at[:, piece], field_all.at[:, piece], sem)]))

    expand(bias_ref, chunk, icols, irows, lines, conv_ref, arrival.wait, 0, emit)
    edges(field_ref[...].reshape(17 * BLOCK, COLS), first_ref, last_ref)
    copies[2].wait()
    copies[3].wait()

    def write(half, group, value):
        chunk[pl.ds(half, 64, stride=2), group, :] = value

    transform(lambda c: planes[c], fcols, frows, write)
    out_ref[...] = chunk[...].astype(out_ref.dtype)
    for copy in results:
        copy.wait()


def last_kernel(
    bias_ref, gathered_ref, icols_all, irows_all, upper_all, lower_all, out_all,
    wide, icols, irows, conv_ref, out_ref, lines, sems, conv_sems, out_sems,
):
    gx, gy = indices()
    copies = fetch(
        [
            (icols_all.at[0, gy], icols, sems.at[0]),
            (irows_all.at[0, gx, :, pl.ds(0, ROWS)], irows, sems.at[1]),
        ]
    )
    arrivals = fetch(
        [
            (upper_all, conv_ref.at[:, pl.ds(0, 64)], conv_sems.at[0]),
            (lower_all, conv_ref.at[:, pl.ds(64, 64)], conv_sems.at[1]),
        ]
    )
    wide[...] = gathered_ref[...].astype(f32)
    copies[0].wait()
    copies[1].wait()
    results = []

    def emit(channel, value):
        out_ref[channel] = value.astype(bf16)
        if channel in ENDS_LAST:
            start = max((e + 1 for e in ENDS_LAST if e < channel), default=0)
            piece = pl.ds(start, channel + 1 - start)
            sem = out_sems.at[len(results)]
            results.extend(fetch([(out_ref.at[piece], out_all.at[piece], sem)]))

    def arrive():
        for copy in arrivals:
            copy.wait()

    expand(bias_ref, wide, icols, irows, lines, conv_ref, arrive, 1, emit)
    for copy in results:
        copy.wait()


vmem = pl.BlockSpec(memory_space=pltpu.VMEM)
smem = pl.BlockSpec(memory_space=pltpu.SMEM)
anywhere = pl.BlockSpec(memory_space=pl.ANY)
hbm = pl.BlockSpec(memory_space=pltpu.HBM)
LIMIT = 56 * 10**6
SMALL = 4 * 10**6
MIDDLE = 55 * 10**6


def call(kernel, outs, args, specs, scratch=(), out_specs=None, flops=10**9, limit=LIMIT, name=None):
    single = not isinstance(outs, (list, tuple))
    if out_specs is None:
        out_specs = vmem if single else [vmem] * len(outs)
    return pl.pallas_call(
        kernel,
        out_shape=outs,
        in_specs=specs,
        out_specs=out_specs,
        scratch_shapes=list(scratch),
        compiler_params=pltpu.CompilerParams(vmem_limit_bytes=limit),
        cost_estimate=pl.CostEstimate(flops=flops, bytes_accessed=4 * 10**6, transcendentals=0),
        name=name,
    )(*args)


def shape_of(dims, kind):
    return jax.ShapeDtypeStruct(dims, kind)


def exchange(value):
    return lax.all_to_all(value, both, split_axis=0, concat_axis=0, tiled=True)


def ring(axis, step):
    size = lax.axis_size(axis)
    return [(i, (i + step) % size) for i in range(size)]


def sides(first, last):
    left = lax.ppermute(last, "gy", ring("gy", 1))
    right = lax.ppermute(first, "gy", ring("gy", -1))
    return left, right


def on_device(grid_field, spectral_weight, conv_near, conv_far, mix_logits, channel_bias):
    grid = grid_field[0]
    mode_weights = jnp.swapaxes(spectral_weight, 3, 4)

    fcols = jnp.asarray(forward_cols())
    plain, wide = forward_rows(0, ROWS), forward_rows(4, 144)
    frows = np.zeros((2,) + wide.shape, wide.dtype)
    frows[0, ..., : 2 * ROWS], frows[1] = plain, wide
    plain, wide = inverse_rows(0, ROWS), inverse_rows(4, 136)
    irows = np.zeros((2,) + wide.shape, wide.dtype)
    irows[0, :, :, :ROWS], irows[1] = plain, wide
    icols = np.stack([inverse_cols()] * 2)
    frows, irows, icols = jnp.asarray(frows), jnp.asarray(irows), jnp.asarray(icols)

    chunks = [shape_of((128, GROUPS, 128), kind) for kind in SUMS]
    answers = [shape_of((128, GROUPS, 128), kind) for kind in MIXED]
    dma = pltpu.SemaphoreType.DMA
    icols_buffer = pltpu.VMEM((2, 64, 2 * COLS), bf16)
    fcols_buffer = pltpu.VMEM((2, COLS, 256), bf16)

    partial, upper, lower = call(
        forward_kernel, [chunks[0]] + [shape_of((C, 8, COLS), bf16)] * 2, (grid, fcols, frows),
        [hbm] * 3,
        (
            pltpu.VMEM((C, ROWS, COLS), bf16), fcols_buffer, pltpu.VMEM((2, 64, 2 * ROWS), bf16),
            dma((4 + GROUPS,)),
        ),
        name="forward",
    )
    top = lax.ppermute(lower, "gx", ring("gx", 1)).reshape(BLOCK, COLS)
    bottom = lax.ppermute(upper, "gx", ring("gx", -1)).reshape(BLOCK, COLS)
    received = exchange(partial)
    tables = [jnp.asarray(t) for t in (spread(3), spread(5), offsets(3), offsets(5))]
    near_shape, far_shape = (BLOCK, 6 * BLOCK), (BLOCK, 10 * BLOCK)
    field, first, last, near_band, far_band = call(
        own_kernel,
        [shape_of((16 * BLOCK, COLS), bf16)] + [shape_of((8, 16 * BLOCK), bf16)] * 2
        + [shape_of(near_shape, bf16), shape_of(far_shape, bf16)],
        (grid, conv_near, conv_far, *tables, upper), [hbm] + [vmem] * 6 + [anywhere],
        (
            pltpu.VMEM((C, ROWS, COLS), bf16), pltpu.VMEM((16 * BLOCK, COLS), bf16),
            dma((GROUPS,)), dma,
        ),
        out_specs=[hbm] + [vmem] * 4, name="own",
    )
    first, last = call(
        edges_kernel, [shape_of((8, 18 * BLOCK), bf16)] * 2, (top, bottom, first, last),
        [vmem] * 4, limit=SMALL, name="edges",
    )

    def mix(layer, received, order):
        return call(
            functools.partial(mix_kernel, layer=layer), [answers[layer], shape_of((8, 128), f32)],
            (mix_logits, received, mode_weights, order), [vmem, vmem, hbm, anywhere],
            (pltpu.VMEM((2, C, 16, C), f32), dma), flops=10**6, limit=SMALL, name="mix",
        )

    def conv(layer, sources, specs, first, count, order):
        return call(
            functools.partial(conv_kernel, layer=layer, first=first, count=count),
            [shape_of((C, 8 * count, COLS), f32), shape_of((8, 128), f32)],
            (mix_logits, *sources, order), [vmem] + specs + [anywhere],
            (
                pltpu.VMEM(((count + 1) * BLOCK, COLS), bf16),
                pltpu.VMEM((C, 8 * count, COLS), f32),
                pltpu.VMEM(near_shape, bf16),
                pltpu.VMEM(far_shape, bf16),
                pltpu.VMEM(((count + 1) * 3 * BLOCK, COLS), bf16),
                pltpu.VMEM(((count + 1) * 5 * BLOCK, COLS), bf16),
                dma((5,)), dma((3,)),
            ),
            out_specs=[hbm, vmem], flops=2 * 10**10, name="conv",
        )

    around = sides(first, last)
    mixed, marker = mix(0, received, mix_logits)
    gathered = exchange(mixed)
    specs = [hbm] * 3 + [vmem] * 2 + [hbm] * 2
    local, _ = conv(0, (field, top, bottom, *around, near_band, far_band), specs, 0, 17, marker)
    field, first, last, partial = call(
        middle_kernel,
        [shape_of((17, BLOCK, COLS), bf16)] + [shape_of((8, 17 * BLOCK), bf16)] * 2 + [chunks[1]],
        (channel_bias, gathered, icols, irows, fcols, frows, local),
        [smem, vmem] + [hbm] * 5,
        (
            pltpu.VMEM((C, 144, COLS), bf16), pltpu.VMEM((128, GROUPS, 128), f32),
            icols_buffer, pltpu.VMEM((2, 136, 128), bf16),
            fcols_buffer, pltpu.VMEM((2, 64, 288), bf16),
            pltpu.VMEM((C, 136, COLS), f32), pltpu.VMEM((17, BLOCK, COLS), bf16),
            pltpu.VMEM((4, 320, 2 * COLS), f32), dma((4,)), dma, dma((2,)),
        ),
        out_specs=[hbm, vmem, vmem, vmem],
        limit=MIDDLE, name="middle",
    )
    received = exchange(partial)
    field, around = field.reshape(17 * BLOCK, COLS), sides(first, last)
    sources, specs = (field, *around, conv_near, conv_far, *tables), [hbm] + [vmem] * 8
    upper, marker = conv(1, sources, specs, 0, 8, mix_logits)
    mixed, marker = mix(1, received, marker)
    gathered = exchange(mixed)
    lower, _ = conv(1, sources, specs, 8, 8, marker)
    result = call(
        last_kernel, shape_of((C, ROWS, COLS), bf16),
        (channel_bias, gathered, icols, irows, upper, lower),
        [smem, vmem] + [hbm] * 4,
        (
            pltpu.VMEM((128, GROUPS, 128), f32), icols_buffer, pltpu.VMEM((2, ROWS, 128), bf16),
            pltpu.VMEM((C, ROWS, COLS), f32), pltpu.VMEM((C, ROWS, COLS), bf16),
            pltpu.VMEM((4, 320, 2 * COLS), f32), dma((2,)), dma((2,)), dma((5,)),
        ),
        out_specs=hbm,
        name="last",
    )
    return result[None]


def solution(mesh):
    in_specs = (
        P(None, None, "gx", "gy"),
        P(None, None, None, None, both),
        P(),
        P(),
        P(),
        P(),
    )
    out_specs = P(None, None, "gx", "gy")
    return jax.shard_map(
        on_device, mesh=mesh, in_specs=in_specs, out_specs=out_specs, check_vma=False
    )
```

```python
import functools
import math

import jax
import jax.numpy as jnp
import ml_dtypes
import numpy as np
from jax import lax
from jax.experimental import pallas as pl
from jax.experimental.pallas import tpu as pltpu
from jax.sharding import PartitionSpec as P

NX = 2048
NY = 2048
C = 20
LAYERS = 2
ROWS = 128
COLS = 256
GROUPS = 5
WIDE = 384
BLOCK = 8 * C

f32 = jnp.float32
bf16 = jnp.bfloat16
both = ("gx", "gy")
SUMS = (jnp.float32, jnp.bfloat16)
MIXED = (jnp.bfloat16, jnp.bfloat16)


def wave(numbers, positions, length):
    product = numbers.astype(np.int64)[:, None] * positions.astype(np.int64)[None, :]
    scale = np.float32(2.0 * math.pi / length)
    angle = (product % length).astype(np.float32) * scale
    angle = angle.astype(np.float64)
    return np.cos(angle).astype(np.float32), np.sin(angle).astype(np.float32)


def halves(value):
    high = value.astype(ml_dtypes.bfloat16)
    low = (value - high.astype(np.float32)).astype(ml_dtypes.bfloat16)
    return high, low


ky_all = np.arange(32)
kx_all = np.concatenate([np.arange(32), np.arange(32) + NX - 32])


def forward_cols():
    cosine, sine = wave(ky_all, np.arange(NY), NY)
    cosine, sine = cosine.T.reshape(NY, 2, 1, 16), sine.T.reshape(NY, 2, 1, 16)
    first = np.stack([cosine, -sine], axis=3)
    second = np.stack([-sine, -cosine], axis=3)
    tables = [np.broadcast_to(t, (NY, 2, 4, 2, 16)).reshape(NY, 256) for t in (first, second)]
    return np.stack(tables).astype(ml_dtypes.bfloat16)


def forward_rows(before, count):
    out = np.zeros((16, 2, 64, 2 * count), ml_dtypes.bfloat16)
    for device in range(16):
        cosine, sine = wave(kx_all, np.arange(ROWS) + device * ROWS, NX)
        table = np.zeros((2, 64, count), np.float32)
        table[0, :, before : before + ROWS] = cosine
        table[1, :, before : before + ROWS] = sine
        high, low = halves(np.transpose(table, (1, 0, 2)).reshape(64, 2 * count))
        out[device, 0], out[device, 1] = high, low
    return out


def inverse_rows(before, count):
    out = np.zeros((16, 2, count, 128), ml_dtypes.bfloat16)
    for device in range(16):
        positions = (np.arange(count) - before + device * ROWS) % NX
        cosine, sine = wave(kx_all, positions, NX)
        high, low = halves(np.concatenate([cosine.T, -sine.T], axis=1))
        out[device, 0], out[device, 1] = high, low
    return out


def inverse_cols():
    width = COLS
    out = np.zeros((8, 2, 64, 2 * width), ml_dtypes.bfloat16)
    weight = (np.where(ky_all == 0, 1.0, 2.0) / (NX * NY)).astype(np.float32)[:, None]
    for device in range(8):
        cosine, sine = wave(ky_all, np.arange(width) + device * COLS, NY)
        cosine, sine = cosine * weight, sine * weight
        real = np.concatenate([cosine, sine], axis=1)
        imaginary = np.concatenate([-sine, cosine], axis=1)
        table = np.stack([real.reshape(2, 16, 2 * width), imaginary.reshape(2, 16, 2 * width)], 1)
        high, low = halves(table.reshape(64, 2 * width))
        out[device, 0], out[device, 1] = high, low
    return out


def spread(taps):
    width = 2 * taps * BLOCK
    lanes = np.arange(width) % (taps * BLOCK) // 8
    return (np.arange(taps * C)[:, None] == lanes[None, :]).astype(ml_dtypes.bfloat16)


def offsets(taps):
    width = 2 * taps * BLOCK
    lanes = np.arange(width)
    place = lanes // (taps * BLOCK) * 8 + lanes % 8
    return (place[None, :] - np.arange(8)[:, None] - 4).astype(np.int32)


def split(value):
    high = value.astype(bf16)
    return high, (value - high.astype(f32)).astype(bf16)


def mul(a, b):
    return jnp.dot(a, b, preferred_element_type=f32)


def fetch(pairs):
    copies = [pltpu.make_async_copy(source, target, sem) for source, target, sem in pairs]
    for copy in copies:
        copy.start()
    return copies


def transform(planes, cols_ref, rows_ref, write):
    lane = lax.broadcasted_iota(jnp.int32, (COLS, 256), 1)
    slot = (lane >> 5) & 3
    zero = jnp.zeros((), bf16)
    rows_high, rows_low = rows_ref[0], rows_ref[1]
    members = jnp.concatenate(
        [
            jnp.concatenate([planes(4 * group + i) for group in range(GROUPS)], axis=0)
            for i in range(4)
        ],
        axis=1,
    )
    sums = []
    for t in range(2):
        placed = [jnp.where(slot == i, cols_ref[t], zero) for i in range(4)]
        sums.append(mul(members, jnp.concatenate(placed, axis=0)))
    count = members.shape[0] // GROUPS
    for group in range(GROUPS):
        own = [total[group * count : group * count + count] for total in sums]
        high, low = split(jnp.concatenate(own, axis=0))
        modes = mul(rows_high, high) + mul(rows_high, low) + mul(rows_low, high)
        for half in range(2):
            write(half, group, modes[:, 128 * half : 128 * half + 128])


def indices():
    return lax.axis_index("gx"), lax.axis_index("gy")


def forward_kernel(
    grid_all, cols_all, rows_all, out_ref, upper_ref, lower_ref, grid_buffer, cols, rows, sems
):
    gx, gy = indices()
    start = pl.multiple_of(gy * COLS, COLS)
    copies = fetch(
        [
            (cols_all.at[:, pl.ds(start, COLS), :], cols, sems.at[0]),
            (rows_all.at[0, gx, :, :, pl.ds(0, 2 * ROWS)], rows, sems.at[1]),
        ]
        + [
            (grid_all.at[pl.ds(4 * g, 4)], grid_buffer.at[pl.ds(4 * g, 4)], sems.at[2 + g])
            for g in range(GROUPS)
        ]
        + [
            (grid_all.at[:, pl.ds(0, 8)], upper_ref, sems.at[2 + GROUPS]),
            (grid_all.at[:, pl.ds(ROWS - 8, 8)], lower_ref, sems.at[3 + GROUPS]),
        ]
    )
    for copy in copies:
        copy.wait()

    def write(half, group, value):
        out_ref[pl.ds(half, 64, stride=2), group, :] = value

    transform(lambda c: grid_buffer[c], cols, rows, write)


def mixture_of(logits_ref, layer):
    exponents = jnp.exp(logits_ref[layer : layer + 1, :])
    weights = exponents / jnp.sum(exponents, axis=1, keepdims=True)
    return [weights[:, i : i + 1] for i in range(3)]


def mix_kernel(logits_ref, received_ref, weights_all, order_ref, out_ref, marker_ref, weights_ref, sem, *, layer):
    (copy,) = fetch([(weights_all.at[layer], weights_ref, sem)])
    total = jnp.sum(received_ref[...].astype(f32), axis=0)
    total = jnp.concatenate([total, jnp.zeros((8 - GROUPS, 128), f32)], axis=0)
    columns = jnp.transpose(total)
    real = jnp.zeros((16, C), f32)
    imaginary = jnp.zeros((16, C), f32)
    copy.wait()
    for c in range(C):
        group, start = c // 4, c % 4 * 32
        in_real = columns[start : start + 16, group : group + 1]
        in_imaginary = columns[start + 16 : start + 32, group : group + 1]
        weight_real, weight_imaginary = weights_ref[0, c], weights_ref[1, c]
        real = real + weight_real * in_real - weight_imaginary * in_imaginary
        imaginary = imaginary + weight_real * in_imaginary + weight_imaginary * in_real
    scale = mixture_of(logits_ref, layer)[0]
    lines = jnp.transpose(jnp.concatenate([real * scale, imaginary * scale] * 4, axis=0))
    lane = lax.broadcasted_iota(jnp.int32, (C, 128), 1)
    row = lax.broadcasted_iota(jnp.int32, (C, 128), 0)
    lines = jnp.where((lane >> 5) == (row & 3), lines, 0.0)
    rows = [jnp.sum(lines[4 * g : 4 * g + 4], axis=0, keepdims=True) for g in range(GROUPS)]
    mixed = jnp.concatenate(rows, axis=0).astype(out_ref.dtype)
    out_ref[...] = jnp.broadcast_to(mixed[None], out_ref.shape)
    marker_ref[...] = lines[:8]


def edge_patterns():
    pick = lax.broadcasted_iota(jnp.int32, (8, COLS), 1) - lax.broadcasted_iota(
        jnp.int32, (8, COLS), 0
    )
    first = jnp.where(pick == 0, 1.0, 0.0).astype(bf16)
    last = jnp.where(pick == COLS - 8, 1.0, 0.0).astype(bf16)
    return first, last


def edge_columns(rows):
    patterns = [p.astype(f32) for p in edge_patterns()]
    patterns = jnp.concatenate(patterns, axis=0).astype(bf16)
    found = lax.dot_general(
        patterns, rows, (((1,), (1,)), ((), ())), preferred_element_type=f32
    )
    return found[:8].astype(bf16), found[8:].astype(bf16)


def edges(rows, first_ref, last_ref):
    first_ref[...], last_ref[...] = edge_columns(rows)


def banded(weights, spread_ref, offsets_ref, steps, width):
    offset = offsets_ref[...][None]
    total = jnp.zeros((C, 8, width), f32)
    taps = len(steps) * C
    for index, step in enumerate(steps):
        own = mul(weights[:, taps * index : taps * index + taps], spread_ref[...])
        total = jnp.where(offset == step, own[:, None, :], total)
    return total.reshape(BLOCK, width).astype(bf16)


NEAR = (-1, 0, 1)
FAR = (-4, -2, 0, 2, 4)
ENDS_LAST = (4, 9, 14, 17, 19)
ENDS = {17: (8, 14, 17), 8: (5, 8)}


def own_kernel(
    grid_all, near_ref, far_ref, near_spread, far_spread, near_offsets, far_offsets, order_ref,
    field_all, first_ref, last_ref, near_band, far_band, grid_ref, field, sems, out_sem,
):
    pieces = [pl.ds(4 * g, 4) for g in range(GROUPS)]
    copies = fetch([(grid_all.at[p], grid_ref.at[p], sems.at[g]) for g, p in enumerate(pieces)])
    near_band[...] = banded(near_ref[0], near_spread, near_offsets, NEAR, 6 * BLOCK)
    far_band[...] = banded(far_ref[0], far_spread, far_offsets, FAR, 10 * BLOCK)
    for copy in copies:
        copy.wait()
    for pair in range(C // 2):
        inner = [grid_ref[2 * pair + i].astype(f32) for i in range(2)]
        for block in range(16):
            value = [v[8 * block : 8 * block + 8] for v in inner]
            place = block * BLOCK + 16 * pair
            field[place : place + 16, :] = jnp.concatenate(value, axis=0).astype(bf16)
    (result,) = fetch([(field, field_all, out_sem)])
    edges(field[...], first_ref, last_ref)
    result.wait()


def edges_kernel(top_ref, bottom_ref, first_ref, last_ref, first_out, last_out):
    found = edge_columns(jnp.concatenate([top_ref[...], bottom_ref[...]], axis=0))
    for own_ref, extra, out_ref in zip((first_ref, last_ref), found, (first_out, last_out)):
        out_ref[:, : C * ROWS] = own_ref[...]
        out_ref[:, C * ROWS :] = extra


def conv_kernel(logits_ref, *refs, layer, first, count):
    if layer == 0:
        main_all, top_all, bottom_all, left_ref, right_ref, near_all, far_all, *refs = refs
        order_ref, out_all, marker_ref, *refs = refs
    else:
        field_all, left_ref, right_ref, near_ref, far_ref, near_spread, far_spread, *refs = refs
        near_offsets, far_offsets, order_ref, out_all, marker_ref, *refs = refs
    field, out_ref, near_band, far_band, near_stack, far_stack, sems, out_sems = refs
    if layer == 0:
        copies = fetch(
            [
                (top_all, field.at[pl.ds(0, BLOCK)], sems.at[0]),
                (main_all, field.at[pl.ds(BLOCK, 16 * BLOCK)], sems.at[1]),
                (bottom_all, field.at[pl.ds(17 * BLOCK, BLOCK)], sems.at[2]),
                (near_all, near_band, sems.at[3]),
                (far_all, far_band, sems.at[4]),
            ]
        )
    else:
        piece = pl.ds(first * BLOCK, (count + 1) * BLOCK)
        copies = fetch([(field_all.at[piece], field, sems.at[0])])
        near_band[...] = banded(near_ref[layer], near_spread, near_offsets, NEAR, 6 * BLOCK)
        far_band[...] = banded(far_ref[layer], far_spread, far_offsets, FAR, 10 * BLOCK)
    lane = lax.broadcasted_iota(jnp.int32, (16, 128), 1)
    row = lax.broadcasted_iota(jnp.int32, (16, 128), 0)
    sides_place = jnp.where(lane == jnp.where(row < 8, row, row + 112), 1.0, 0.0).astype(bf16)
    lanes = slice(first * BLOCK, (first + count + 1) * BLOCK)
    sides = [r[:, lanes].astype(f32) for r in (right_ref, left_ref)]
    sides = jnp.concatenate(sides, axis=0)
    side = lax.dot_general(
        sides.astype(bf16), sides_place, (((0,), (0,)), ((), ())), preferred_element_type=f32
    )
    side = side.astype(bf16)
    for copy in copies:
        copy.wait()

    def side_of(block):
        start = block * BLOCK
        if layer == 0:
            start = {0: 16 * BLOCK, 17: 17 * BLOCK}.get(block, start - BLOCK)
        return side[start : start + BLOCK]

    _, near_scale, far_scale = mixture_of(logits_ref, layer)
    results = []
    for index in range(count + 1):
        rows = slice(index * BLOCK, index * BLOCK + BLOCK)
        block = jnp.concatenate([field[rows, :], side_of(index)], axis=1)
        moved = {0: block}
        for step in (-4, -2, -1, 1, 2, 4):
            moved[step] = pltpu.roll(block, (-step) % WIDE, 1)
        for steps, stack in ((NEAR, near_stack), (FAR, far_stack)):
            for position, step in enumerate(steps):
                start = (index * len(steps) + position) * BLOCK
                stack[start : start + BLOCK, :] = moved[step][:, :COLS]
        if index == 0:
            continue
        done = index - 1
        near_rows = near_stack[done * 3 * BLOCK : (done + 2) * 3 * BLOCK, :]
        far_rows = far_stack[done * 5 * BLOCK : (done + 2) * 5 * BLOCK, :]
        total = near_scale * mul(near_band[...], near_rows) + far_scale * mul(
            far_band[...], far_rows
        )
        out_ref[:, 8 * done : 8 * done + 8, :] = total.reshape(C, 8, COLS)
        if done + 1 in ENDS[count]:
            start = max((e for e in ENDS[count] if e < done + 1), default=0)
            piece = pl.ds(8 * start, 8 * (done + 1 - start))
            results += fetch(
                [(out_ref.at[:, piece], out_all.at[:, piece], out_sems.at[len(results)])]
            )
    marker_ref[...] = total[:8, :128]
    for copy in results:
        copy.wait()


def gelu(value):
    return 0.5 * value * (1.0 + lax.erf(value * math.sqrt(0.5)))


def expand(bias_ref, gathered, cols, rows, lines, conv_ref, arrive, layer, emit):
    parts = []
    for group in range(GROUPS):
        pair = [gathered[pl.ds(half, 64, stride=2), group, :] for half in range(2)]
        parts.append(jnp.concatenate(pair, axis=1))
    high, low = split(jnp.concatenate(parts, axis=0))
    stacked = jnp.concatenate([high, low], axis=0)
    rows_high, rows_low = rows[0], rows[1]
    rows_twice = jnp.concatenate([rows_high, rows_high], axis=1)
    empty = jnp.zeros((32, 2 * COLS), bf16)
    for slot in range(4):
        placed = []
        for t in range(2):
            table = cols[t]
            pieces = []
            for half in range(2):
                own = table[32 * half : 32 * half + 32]
                pieces += [own if i == slot else empty for i in range(4)]
            placed.append(jnp.concatenate(pieces, axis=0))
        first = mul(stacked, placed[0])
        lines[slot] = first[:320] + first[320:] + mul(high, placed[1])
    arrive()
    for channel in range(C):
        group, slot = channel // 4, channel % 4
        here = lines[slot, 64 * group : 64 * group + 64]
        line_high, line_low = split(jnp.concatenate([here[:, :COLS], here[:, COLS:]], axis=0))
        value = mul(rows_twice, jnp.concatenate([line_high, line_low], axis=0)) + mul(
            rows_low, line_high
        )
        emit(channel, gelu(value + conv_ref[channel] + bias_ref[layer, channel]))


def middle_kernel(
    bias_ref, gathered_ref, icols_all, irows_all, fcols_all, frows_all, conv_all,
    field_all, first_ref, last_ref, out_ref,
    planes, chunk, icols, irows, fcols, frows, conv_ref, field_ref, lines, sems, conv_sem,
    field_sems,
):
    gx, gy = indices()
    start = pl.multiple_of(gy * COLS, COLS)
    copies = fetch(
        [
            (icols_all.at[0, gy], icols, sems.at[0]),
            (irows_all.at[1, gx], irows, sems.at[1]),
            (fcols_all.at[:, pl.ds(start, COLS), :], fcols, sems.at[2]),
            (frows_all.at[1, gx], frows, sems.at[3]),
        ]
    )
    (arrival,) = fetch([(conv_all, conv_ref, conv_sem)])
    chunk[...] = gathered_ref[...].astype(f32)
    copies[0].wait()
    copies[1].wait()
    waiting = []
    results = []

    def emit(channel, value):
        rounded = value.astype(bf16)
        planes[channel, :136] = rounded
        planes[channel, 136:] = jnp.zeros((8, COLS), bf16)
        waiting.append(rounded.astype(f32))
        if channel % 2 == 1:
            for block in range(17):
                rows = slice(8 * block, 8 * block + 8)
                both_rows = jnp.concatenate([waiting[0][rows], waiting[1][rows]], axis=0)
                place = 8 * (channel - 1)
                field_ref[block, place : place + 16, :] = both_rows.astype(bf16)
            waiting.clear()
        if channel in (9, 19):
            piece = pl.ds(8 * (channel - 9), 80)
            sem = field_sems.at[len(results)]
            results.extend(fetch([(field_ref.at[:, piece], field_all.at[:, piece], sem)]))

    expand(bias_ref, chunk, icols, irows, lines, conv_ref, arrival.wait, 0, emit)
    edges(field_ref[...].reshape(17 * BLOCK, COLS), first_ref, last_ref)
    copies[2].wait()
    copies[3].wait()

    def write(half, group, value):
        chunk[pl.ds(half, 64, stride=2), group, :] = value

    transform(lambda c: planes[c], fcols, frows, write)
    out_ref[...] = chunk[...].astype(out_ref.dtype)
    for copy in results:
        copy.wait()


def last_kernel(
    bias_ref, gathered_ref, icols_all, irows_all, upper_all, lower_all, out_all,
    wide, icols, irows, conv_ref, out_ref, lines, sems, conv_sems, out_sems,
):
    gx, gy = indices()
    copies = fetch(
        [
            (icols_all.at[0, gy], icols, sems.at[0]),
            (irows_all.at[0, gx, :, pl.ds(0, ROWS)], irows, sems.at[1]),
        ]
    )
    arrivals = fetch(
        [
            (upper_all, conv_ref.at[:, pl.ds(0, 64)], conv_sems.at[0]),
            (lower_all, conv_ref.at[:, pl.ds(64, 64)], conv_sems.at[1]),
        ]
    )
    wide[...] = gathered_ref[...].astype(f32)
    copies[0].wait()
    copies[1].wait()
    results = []

    def emit(channel, value):
        out_ref[channel] = value.astype(bf16)
        if channel in ENDS_LAST:
            start = max((e + 1 for e in ENDS_LAST if e < channel), default=0)
            piece = pl.ds(start, channel + 1 - start)
            sem = out_sems.at[len(results)]
            results.extend(fetch([(out_ref.at[piece], out_all.at[piece], sem)]))

    def arrive():
        for copy in arrivals:
            copy.wait()

    expand(bias_ref, wide, icols, irows, lines, conv_ref, arrive, 1, emit)
    for copy in results:
        copy.wait()


vmem = pl.BlockSpec(memory_space=pltpu.VMEM)
smem = pl.BlockSpec(memory_space=pltpu.SMEM)
anywhere = pl.BlockSpec(memory_space=pl.ANY)
hbm = pl.BlockSpec(memory_space=pltpu.HBM)
LIMIT = 56 * 10**6
SMALL = 4 * 10**6
MIDDLE = 55 * 10**6
FORWARD = 55 * 10**6


def call(kernel, outs, args, specs, scratch=(), out_specs=None, flops=10**9, limit=LIMIT, name=None):
    single = not isinstance(outs, (list, tuple))
    if out_specs is None:
        out_specs = vmem if single else [vmem] * len(outs)
    return pl.pallas_call(
        kernel,
        out_shape=outs,
        in_specs=specs,
        out_specs=out_specs,
        scratch_shapes=list(scratch),
        compiler_params=pltpu.CompilerParams(vmem_limit_bytes=limit),
        cost_estimate=pl.CostEstimate(flops=flops, bytes_accessed=4 * 10**6, transcendentals=0),
        name=name,
    )(*args)


def shape_of(dims, kind):
    return jax.ShapeDtypeStruct(dims, kind)


def exchange(value):
    return lax.all_to_all(value, both, split_axis=0, concat_axis=0, tiled=True)


def ring(axis, step):
    size = lax.axis_size(axis)
    return [(i, (i + step) % size) for i in range(size)]


def sides(first, last):
    left = lax.ppermute(last, "gy", ring("gy", 1))
    right = lax.ppermute(first, "gy", ring("gy", -1))
    return left, right


def on_device(grid_field, spectral_weight, conv_near, conv_far, mix_logits, channel_bias):
    grid = grid_field[0]
    mode_weights = jnp.swapaxes(spectral_weight, 3, 4)

    fcols = jnp.asarray(forward_cols())
    plain, wide = forward_rows(0, ROWS), forward_rows(4, 144)
    frows = np.zeros((2,) + wide.shape, wide.dtype)
    frows[0, ..., : 2 * ROWS], frows[1] = plain, wide
    plain, wide = inverse_rows(0, ROWS), inverse_rows(4, 136)
    irows = np.zeros((2,) + wide.shape, wide.dtype)
    irows[0, :, :, :ROWS], irows[1] = plain, wide
    icols = np.stack([inverse_cols()] * 2)
    frows, irows, icols = jnp.asarray(frows), jnp.asarray(irows), jnp.asarray(icols)

    chunks = [shape_of((128, GROUPS, 128), kind) for kind in SUMS]
    answers = [shape_of((128, GROUPS, 128), kind) for kind in MIXED]
    dma = pltpu.SemaphoreType.DMA
    icols_buffer = pltpu.VMEM((2, 64, 2 * COLS), bf16)
    fcols_buffer = pltpu.VMEM((2, COLS, 256), bf16)

    partial, upper, lower = call(
        forward_kernel, [chunks[0]] + [shape_of((C, 8, COLS), bf16)] * 2, (grid, fcols, frows),
        [hbm] * 3,
        (
            pltpu.VMEM((C, ROWS, COLS), bf16), fcols_buffer, pltpu.VMEM((2, 64, 2 * ROWS), bf16),
            dma((4 + GROUPS,)),
        ),
        limit=FORWARD, name="forward",
    )
    top = lax.ppermute(lower, "gx", ring("gx", 1)).reshape(BLOCK, COLS)
    bottom = lax.ppermute(upper, "gx", ring("gx", -1)).reshape(BLOCK, COLS)
    received = exchange(partial)
    tables = [jnp.asarray(t) for t in (spread(3), spread(5), offsets(3), offsets(5))]
    near_shape, far_shape = (BLOCK, 6 * BLOCK), (BLOCK, 10 * BLOCK)
    field, first, last, near_band, far_band = call(
        own_kernel,
        [shape_of((16 * BLOCK, COLS), bf16)] + [shape_of((8, 16 * BLOCK), bf16)] * 2
        + [shape_of(near_shape, bf16), shape_of(far_shape, bf16)],
        (grid, conv_near, conv_far, *tables, upper), [hbm] + [vmem] * 6 + [anywhere],
        (
            pltpu.VMEM((C, ROWS, COLS), bf16), pltpu.VMEM((16 * BLOCK, COLS), bf16),
            dma((GROUPS,)), dma,
        ),
        out_specs=[hbm] + [vmem] * 4, name="own",
    )
    first, last = call(
        edges_kernel, [shape_of((8, 18 * BLOCK), bf16)] * 2, (top, bottom, first, last),
        [vmem] * 4, limit=SMALL, name="edges",
    )

    def mix(layer, received, order):
        return call(
            functools.partial(mix_kernel, layer=layer), [answers[layer], shape_of((8, 128), f32)],
            (mix_logits, received, mode_weights, order), [vmem, vmem, hbm, anywhere],
            (pltpu.VMEM((2, C, 16, C), f32), dma), flops=10**6, limit=SMALL, name="mix",
        )

    def conv(layer, sources, specs, first, count, order):
        return call(
            functools.partial(conv_kernel, layer=layer, first=first, count=count),
            [shape_of((C, 8 * count, COLS), f32), shape_of((8, 128), f32)],
            (mix_logits, *sources, order), [vmem] + specs + [anywhere],
            (
                pltpu.VMEM(((count + 1) * BLOCK, COLS), bf16),
                pltpu.VMEM((C, 8 * count, COLS), f32),
                pltpu.VMEM(near_shape, bf16),
                pltpu.VMEM(far_shape, bf16),
                pltpu.VMEM(((count + 1) * 3 * BLOCK, COLS), bf16),
                pltpu.VMEM(((count + 1) * 5 * BLOCK, COLS), bf16),
                dma((5,)), dma((3,)),
            ),
            out_specs=[hbm, vmem], flops=2 * 10**10, name="conv",
        )

    around = sides(first, last)
    mixed, marker = mix(0, received, mix_logits)
    gathered = exchange(mixed)
    specs = [hbm] * 3 + [vmem] * 2 + [hbm] * 2
    local, _ = conv(0, (field, top, bottom, *around, near_band, far_band), specs, 0, 17, marker)
    field, first, last, partial = call(
        middle_kernel,
        [shape_of((17, BLOCK, COLS), bf16)] + [shape_of((8, 17 * BLOCK), bf16)] * 2 + [chunks[1]],
        (channel_bias, gathered, icols, irows, fcols, frows, local),
        [smem, vmem] + [hbm] * 5,
        (
            pltpu.VMEM((C, 144, COLS), bf16), pltpu.VMEM((128, GROUPS, 128), f32),
            icols_buffer, pltpu.VMEM((2, 136, 128), bf16),
            fcols_buffer, pltpu.VMEM((2, 64, 288), bf16),
            pltpu.VMEM((C, 136, COLS), f32), pltpu.VMEM((17, BLOCK, COLS), bf16),
            pltpu.VMEM((4, 320, 2 * COLS), f32), dma((4,)), dma, dma((2,)),
        ),
        out_specs=[hbm, vmem, vmem, vmem],
        limit=MIDDLE, name="middle",
    )
    received = exchange(partial)
    field, around = field.reshape(17 * BLOCK, COLS), sides(first, last)
    sources, specs = (field, *around, conv_near, conv_far, *tables), [hbm] + [vmem] * 8
    upper, marker = conv(1, sources, specs, 0, 8, mix_logits)
    mixed, marker = mix(1, received, marker)
    gathered = exchange(mixed)
    lower, _ = conv(1, sources, specs, 8, 8, marker)
    result = call(
        last_kernel, shape_of((C, ROWS, COLS), bf16),
        (channel_bias, gathered, icols, irows, upper, lower),
        [smem, vmem] + [hbm] * 4,
        (
            pltpu.VMEM((128, GROUPS, 128), f32), icols_buffer, pltpu.VMEM((2, ROWS, 128), bf16),
            pltpu.VMEM((C, ROWS, COLS), f32), pltpu.VMEM((C, ROWS, COLS), bf16),
            pltpu.VMEM((4, 320, 2 * COLS), f32), dma((2,)), dma((2,)), dma((5,)),
        ),
        out_specs=hbm,
        name="last",
    )
    return result[None]


def solution(mesh):
    in_specs = (
        P(None, None, "gx", "gy"),
        P(None, None, None, None, both),
        P(),
        P(),
        P(),
        P(),
    )
    out_specs = P(None, None, "gx", "gy")
    return jax.shard_map(
        on_device, mesh=mesh, in_specs=in_specs, out_specs=out_specs, check_vma=False
    )
```
